1024 devices in a mesh: seq: 128 (over y, x, core), chan: 8 (over z).
Axes of the slice: x: 8, y: 8, z: 8, core: 2. Of those that a mesh axis runs over, the one named last changes fastest.
Arguments:
- q_in: bfloat16 [16384, 4096], P('seq', 'chan'), may hold values from -6 to 6
- k_in: bfloat16 [16384, 4096], P('seq', 'chan'), may hold values from -6 to 6
- v_in: bfloat16 [16384, 4096], P('seq', 'chan'), may hold values from -6 to 6
- short_filters: float32 [3, 3, 4096], P(None, None, 'chan'), may hold values from -3.5 to 3.5
- long_filter: float32 [8, 512, 16384], P('chan', 'seq'), may hold values from -8 to 8
- out_weight: bfloat16 [4096, 4096], P('chan'), may hold values from -0.09375 to 0.09375
- out_grad: bfloat16 [16384, 4096], P('seq', 'chan'), may hold values from -0.059814453 to 0.059814453
Outputs:
- operator_out: bfloat16 [16384, 4096], P('seq', 'chan')
- filter_grad: float32 [8, 512, 16384], P('chan', 'seq')
The draws below stay inside these ranges and needn't reach their ends.
All inputs are finite; a program needn't handle non-finite values.
Results may differ from the reference program's by a relative error of at most 0.0058.
Values may be sent and summed in bfloat16 or wider, within the bound.
No kernel may reach another device: no remote copies, remote signals or barrier semaphores. Data moves between devices by JAX's collectives and lax.ppermute only.
A program may use at most 32 MiB of HBM per device.

```python
import math
import jax
import jax.numpy as jnp
from jax import lax

D = 4096
TAPS = 3
LEN = 16384
GROUPS = 8
GROUP_W = 512


def draw_long_filter(key, part):
    rate_key, noise_key = jax.random.split(jax.random.fold_in(key, 17))
    shape = (GROUPS, GROUP_W, LEN)
    rate = jnp.exp(jax.random.uniform(rate_key, (GROUPS, GROUP_W, 1), jnp.float32, math.log(0.5), math.log(600.0)))
    noise = jnp.clip(jax.random.normal(noise_key, shape, jnp.float32), -4.0, 4.0)
    place = jnp.arange(LEN, dtype=jnp.float32)[None, None, :] / LEN
    amplitude = jnp.sqrt(2.0 * rate / LEN)
    return jnp.clip(amplitude * jnp.exp(-rate * place) * noise, -8.0, 8.0).astype(jnp.float32)


def level_of(stream_key, dims, cuts, smallest, high):
    def one(axis_at, shards_of):
        heights = jax.random.uniform(jax.random.fold_in(jax.random.fold_in(stream_key, 6), axis_at), (shards_of,), jnp.float32, smallest / len(cuts), high / len(cuts))
        return jnp.repeat(jnp.exp(heights), dims[axis_at] // shards_of).reshape((-1,) + (1,) * (len(dims) - axis_at - 1))

    gain = one(*cuts[0])
    for cut in cuts[1:]:
        gain = gain * one(*cut)
    return gain


def gaussian(key, extent, deviation, bound, cuts=(), kind=jnp.bfloat16):
    loudness = level_of(key, extent, cuts, -0.22, 0.18) if cuts else 1.0
    array = jax.random.normal(key, extent, jnp.float32) * deviation * loudness
    return jnp.minimum(jnp.maximum(array, -bound), bound).astype(kind)


def setup_inputs(seed: int = 0) -> dict:
    splits = jax.random.split(jax.random.key(seed), 8)
    return {
        "q_in": gaussian(splits[0], (LEN, D), 1.0, 6.0, ((0, 128), (1, 8))),
        "k_in": gaussian(splits[1], (LEN, D), 1.0, 6.0, ((0, 128), (1, 8))),
        "v_in": gaussian(splits[2], (LEN, D), 1.0, 6.0, ((0, 128), (1, 8))),
        "short_filters": gaussian(splits[3], (3, TAPS, D), TAPS ** -0.5, 3.5, ((2, 8),), jnp.float32),
        "long_filter": draw_long_filter(jax.random.fold_in(splits[7], 71), 0),
        "out_weight": gaussian(splits[5], (D, D), D ** -0.5, 0.09375, ((0, 8),)),
        "out_grad": gaussian(splits[6], (LEN, D), 0.01, 0.059814453, ((0, 128), (1, 8))),
    }


def short_conv(stream, taps):
    count = taps.shape[0]
    length = stream.shape[0]
    padded = jnp.concatenate((jnp.zeros((count - 1, stream.shape[1]), jnp.float32), stream), axis=0)
    result = jnp.zeros_like(stream)
    for lag in range(count):
        result = result + taps[lag][None, :] * padded[count - 1 - lag:count - 1 - lag + length]
    return result


def reference(q_in, k_in, v_in, short_filters, long_filter, out_weight, out_grad):
    q_conv = short_conv(q_in.astype(jnp.float32), short_filters[0])
    k_conv = short_conv(k_in.astype(jnp.float32), short_filters[1])
    v_conv = short_conv(v_in.astype(jnp.float32), short_filters[2])
    gated = lax.optimization_barrier((k_conv * v_conv).astype(jnp.bfloat16))
    grad_gate = jnp.dot(out_grad, out_weight.T, preferred_element_type=jnp.float32)
    dy_gate = lax.optimization_barrier((grad_gate * q_conv).astype(jnp.bfloat16))
    total = 2 * LEN
    z_groups = gated.astype(jnp.float32).T.reshape(GROUPS, GROUP_W, LEN)
    d_groups = dy_gate.astype(jnp.float32).T.reshape(GROUPS, GROUP_W, LEN)

    def one_group(items):
        z_part, h_part, d_part = items
        z_spec = jnp.fft.rfft(z_part, n=total, axis=1)
        h_spec = jnp.fft.rfft(h_part, n=total, axis=1)
        d_spec = jnp.fft.rfft(d_part, n=total, axis=1)
        y_part = jnp.fft.irfft(z_spec * h_spec, n=total, axis=1)[:, :LEN].astype(jnp.bfloat16)
        h_grad = jnp.fft.irfft(jnp.conj(z_spec) * d_spec, n=total, axis=1)[:, :LEN].astype(jnp.float32)
        return y_part, h_grad

    y_groups, filter_grad = lax.map(one_group, (z_groups, long_filter, d_groups))
    y_long = lax.optimization_barrier(y_groups.reshape(D, LEN).T)
    operator_out = (q_conv * y_long.astype(jnp.float32)).astype(jnp.bfloat16)
    return operator_out, filter_grad
```

```python
import jax
import jax.numpy as jnp
from jax import lax
from jax.experimental import pallas as pl
from jax.experimental.pallas import tpu as pltpu
from jax.sharding import PartitionSpec as P

F32 = jnp.float32
BF16 = jnp.bfloat16
B = 128
HALF = 64
PAIR = 2 * B
CH = 4
STRIP = B * B + B
STEP = 16
STRIP_SPEC = pl.BlockSpec((1, B, STRIP), lambda c: (c, 0, 0))
NT = (((1,), (1,)), ((), ()))


def iota2(shape, dim):
    return lax.broadcasted_iota(jnp.int32, shape, dim)


def spread_kernel(k_ref, v_ref, o_ref):
    row, col = iota2((PAIR, PAIR), 0), iota2((PAIR, PAIR), 1)
    source = (row // CH) % 2 * B + row // (2 * CH) * CH + row % CH
    pick = (col == source).astype(BF16)
    for g in range(4):
        lanes = slice(B * g, B * g + B)
        both = jnp.concatenate((k_ref[:, lanes], v_ref[:, lanes]), axis=1)
        rows = lax.dot_general(pick, both, NT, preferred_element_type=F32)
        o_ref[PAIR * g : PAIR * g + PAIR, :] = rows.astype(BF16)


def spread(k, v):
    return pl.pallas_call(
        spread_kernel, out_shape=jax.ShapeDtypeStruct((8 * B, B), BF16), name="spread"
    )(k, v)


def build_strip(tall, strip_ref):
    near = iota2((B, B), 1) < B - iota2((B, B), 0)

    def step(i, carry):
        base = pl.multiple_of(8 * i, 8)
        now = tall[pl.ds(base + 8, 8), :]
        last = tall[pl.ds(base, 8), :]
        for j in range(8):
            this = jnp.broadcast_to(now[j : j + 1, :], (B, B))
            prior = last[7:8, :] if j == 0 else now[j - 1 : j, :]
            mixed = jnp.where(near, this, jnp.broadcast_to(prior, (B, B)))
            tile = pltpu.roll(mixed, 0, 1, stride=1, stride_axis=0)
            at = pl.multiple_of(B * (8 * i + j + 1), B)
            strip_ref[0, :, pl.ds(at, B)] = tile.astype(BF16)
        return carry

    strip_ref[0, :, 0:B] = jnp.zeros((B, B), BF16)
    lax.fori_loop(0, B // 8, step, 0)


def strip_kernel(x_ref, strip_ref, tall):
    tall[0:8, :] = jnp.zeros((8, B), F32)
    tall[8 : 8 + B, :] = x_ref[0]
    build_strip(tall, strip_ref)


def strips(x, name):
    return pl.pallas_call(
        strip_kernel,
        grid=(CH,),
        in_specs=[pl.BlockSpec((1, B, B), lambda c: (c, 0, 0))],
        out_specs=STRIP_SPEC,
        out_shape=pltpu.HBM((CH, B, STRIP), BF16),
        scratch_shapes=[pltpu.VMEM((8 + B, B), F32)],
        compiler_params=pltpu.CompilerParams(vmem_limit_bytes=16 << 20),
        cost_estimate=pl.CostEstimate(
            flops=5 * 10**9, transcendentals=0, bytes_accessed=2 * CH * B * STRIP
        ),
        name=name,
    )(x)


def pair_conv(even, odd, strip_ref, xs, xa, acc):
    xs[0, 0:STEP, :] = jnp.zeros((STEP, B), F32)
    xs[1, 0:STEP, :] = jnp.zeros((STEP, B), F32)
    xs[0, STEP : STEP + HALF, :] = even
    xs[1, STEP : STEP + HALF, :] = odd
    for j in range(STEP):
        at = slice(STEP - j, STEP - j + HALF)
        xa[:, PAIR * j : PAIR * j + B] = xs[0, at, :].astype(BF16)
        xa[:, PAIR * j + B : PAIR * j + PAIR] = xs[1, at, :].astype(BF16)
    for i in range(HALF // STEP):
        right = []
        for e in range(STEP * i, STEP * i + STEP):
            right.append(strip_ref[0, :, PAIR * e + B : PAIR * e + B + PAIR])
            right.append(strip_ref[0, :, PAIR * e : PAIR * e + PAIR])
        out = jnp.dot(
            xa[0 : HALF - STEP * i, :],
            jnp.concatenate(right, axis=0),
            preferred_element_type=F32,
        )
        if i == 0:
            acc[...] = out
        else:
            acc[STEP * i : HALF, :] += out


CONV_SCRATCH = [
    pltpu.VMEM((2, STEP + HALF, B), F32),
    pltpu.VMEM((HALF, PAIR * STEP), BF16),
    pltpu.VMEM((HALF, PAIR), F32),
]


def long_kernel(w_ref, kv_ref, strip_ref, y_ref, g_ref, kvf, yf, xs, xa, acc):
    c = pl.program_id(0)

    @pl.when(c == 0)
    def _():
        kvf[...] = kv_ref[...].astype(F32)

    row, lane = iota2((B, B), 0), iota2((B, B), 1)

    def short(stream):
        x = kvf[pl.ds(CH * stream + c, B, stride=2 * CH), :]
        before = jnp.where(row == 0, 0.0, pltpu.roll(x, 1, 0))
        out = w_ref[(stream + 1) * 12 + c] * x
        for lag in (1, 2):
            moved = pltpu.roll(jnp.where(lane < B - lag, x, before), lag, 1)
            out = out + w_ref[(stream + 1) * 12 + CH * lag + c] * moved
        return out

    g_ref[0] = (short(0) * short(1)).astype(BF16).astype(F32)
    even = g_ref[0, pl.ds(0, HALF, stride=2), :]
    odd = g_ref[0, pl.ds(1, HALF, stride=2), :]
    pair_conv(even, odd, strip_ref, xs, xa, acc)
    yf[pl.ds(c, HALF, stride=2 * CH), :] = acc[:, 0:B]
    yf[pl.ds(CH + c, HALF, stride=2 * CH), :] = acc[:, B:PAIR]

    @pl.when(c == CH - 1)
    def _():
        y_ref[...] = yf[...].astype(BF16)


def long_conv(w, kv, strip):
    return pl.pallas_call(
        long_kernel,
        grid=(CH,),
        in_specs=[
            pl.BlockSpec(memory_space=pltpu.SMEM),
            pl.BlockSpec((8 * B, B), lambda c: (0, 0)),
            STRIP_SPEC,
        ],
        out_specs=[
            pl.BlockSpec((CH * B, B), lambda c: (0, 0)),
            pl.BlockSpec((1, B, B), lambda c: (c, 0, 0)),
        ],
        out_shape=[
            jax.ShapeDtypeStruct((CH * B, B), BF16),
            jax.ShapeDtypeStruct((CH, B, B), F32),
        ],
        scratch_shapes=[
            pltpu.VMEM((8 * B, B), F32),
            pltpu.VMEM((CH * B, B), F32),
            *CONV_SCRATCH,
        ],
        compiler_params=pltpu.CompilerParams(vmem_limit_bytes=20 << 20),
        cost_estimate=pl.CostEstimate(
            flops=5 * 10**9, transcendentals=0, bytes_accessed=2 * CH * B * STRIP
        ),
        name="long_conv",
    )(w, kv, pltpu.with_memory_space_constraint(strip, pltpu.HBM))


def flip(x, precision=None):
    n = x.shape[0]
    rows = (iota2((n, n), 0) + iota2((n, n), 1) == n - 1).astype(x.dtype)
    cols = (iota2((B, B), 0) + iota2((B, B), 1) == B - 1).astype(x.dtype)
    half = jnp.dot(rows, x, preferred_element_type=F32, precision=precision).astype(x.dtype)
    return jnp.dot(half, cols, preferred_element_type=F32, precision=precision)


def grad_kernel(back_ref, q_ref, strip_ref, o_ref, f_ref, backf, yf, xs, xa, acc):
    c = pl.program_id(0)

    @pl.when(c == 0)
    def _():
        backf[...] = back_ref[...].astype(F32)

    yf[pl.ds(c, B, stride=CH), :] = backf[pl.ds(c, B, stride=2 * CH), :]
    first = backf[pl.ds(3 * CH + c, HALF, stride=4 * CH), :]
    second = backf[pl.ds(CH + c, HALF, stride=4 * CH), :]
    even, odd = flip(first.astype(BF16)), flip(second.astype(BF16))
    pair_conv(even, odd, strip_ref, xs, xa, acc)
    exact = lax.Precision.HIGHEST
    f_ref[0, pl.ds(0, HALF, stride=2), :] = flip(acc[:, B:PAIR], exact)
    f_ref[0, pl.ds(1, HALF, stride=2), :] = flip(acc[:, 0:B], exact)

    @pl.when(c == CH - 1)
    def _():
        for g in range(CH):
            part = slice(B * g, B * g + B)
            o_ref[:, part] = (yf[part, :] * q_ref[part, :]).T.astype(BF16)


def grad_conv(back, q_conv_t, strip):
    return pl.pallas_call(
        grad_kernel,
        grid=(CH,),
        in_specs=[
            pl.BlockSpec((8 * B, B), lambda c: (0, 0)),
            pl.BlockSpec((CH * B, B), lambda c: (0, 0)),
            STRIP_SPEC,
        ],
        out_specs=[
            pl.BlockSpec((B, CH * B), lambda c: (0, 0)),
            pl.BlockSpec((1, B, B), lambda c: (c, 0, 0)),
        ],
        out_shape=[
            jax.ShapeDtypeStruct((B, CH * B), BF16),
            jax.ShapeDtypeStruct((CH, B, B), F32),
        ],
        scratch_shapes=[
            pltpu.VMEM((8 * B, B), F32),
            pltpu.VMEM((CH * B, B), F32),
            *CONV_SCRATCH,
        ],
        compiler_params=pltpu.CompilerParams(vmem_limit_bytes=20 << 20),
        cost_estimate=pl.CostEstimate(
            flops=5 * 10**9, transcendentals=0, bytes_accessed=2 * CH * B * STRIP
        ),
        name="grad_conv",
    )(back, q_conv_t, pltpu.with_memory_space_constraint(strip, pltpu.HBM))


def project_kernel(at_ref, w_ref, a_ref, b_ref, c_ref, d_ref, e_ref, q_ref, y_ref, o_ref, df, yf, of):
    width = a_ref.shape[1]
    tokens = a_ref.shape[0]
    total = None
    blocks = [a_ref[...], b_ref[...]]
    for ref in (c_ref, d_ref, e_ref):
        blocks += [ref[0:tokens, :], ref[tokens : 2 * tokens, :]]
    for k, block in enumerate(blocks):
        start = pl.multiple_of(at_ref[k] * width, B)
        part = lax.dot_general(w_ref[:, pl.ds(start, width)], block, NT, preferred_element_type=F32)
        total = part if total is None else total + part
    df[...] = total * q_ref[...]
    yf[...] = y_ref[...].astype(F32)
    for c in range(CH):
        of[pl.ds(c, B, stride=2 * CH), :] = yf[pl.ds(c, B, stride=CH), :]
        of[pl.ds(CH + c, B, stride=2 * CH), :] = df[pl.ds(c, B, stride=CH), :]
    o_ref[...] = of[...].astype(BF16)


def project(order, weight, blocks, q_conv_t, y):
    vmem = pl.BlockSpec(memory_space=pltpu.VMEM)
    return pl.pallas_call(
        project_kernel,
        in_specs=[pl.BlockSpec(memory_space=pltpu.SMEM)] + [vmem] * 8,
        out_specs=vmem,
        out_shape=jax.ShapeDtypeStruct((8 * B, B), BF16),
        scratch_shapes=[
            pltpu.VMEM((CH * B, B), F32),
            pltpu.VMEM((CH * B, B), F32),
            pltpu.VMEM((8 * B, B), F32),
        ],
        compiler_params=pltpu.CompilerParams(vmem_limit_bytes=16 << 20),
        cost_estimate=pl.CostEstimate(flops=10**9, transcendentals=0, bytes_accessed=5 * 2**20),
        name="project",
    )(order, weight, *blocks, q_conv_t, y)


INNER = [(i, i ^ 1) for i in range(8)]
OUTER = [(i, (i + 1 if i % 2 else i - 1) % 8) for i in range(8)]


def swap_order():
    own = [[i] for i in range(8)]
    first = [own[i ^ 1] for i in range(8)]
    second = [own[j] + first[j] for _, j in OUTER]
    third = [second[j] for _, j in INNER]
    fourth = [third[j] for _, j in OUTER]
    return [sum(parts, []) for parts in zip(own, first, second, third, fourth, strict=True)]


def exchange(value, axis):
    return lax.all_to_all(value, axis, split_axis=0, concat_axis=0, tiled=True)


def on_device(q_in, k_in, v_in, short_filters, long_filter, out_weight, out_grad):
    tokens, width = q_in.shape
    seq = lax.axis_size("seq")
    z = lax.axis_index("chan")
    tie = lax.optimization_barrier
    r1 = lax.ppermute(out_grad, "chan", INNER)
    kv = spread(k_in, v_in)
    kv, r1 = tie((kv, r1))
    pair = jnp.concatenate((out_grad, r1), axis=0)
    r2 = lax.ppermute(pair, "chan", OUTER)
    kv = exchange(kv.reshape(seq, 2 * CH, tokens), "seq")
    r2, q_in, long_filter = tie((r2, q_in, long_filter))
    r3 = lax.ppermute(r2, "chan", INNER)
    r4 = lax.ppermute(r3, "chan", OUTER)
    homes = lax.dynamic_index_in_dim(jnp.array(swap_order(), jnp.int32), z, 0, keepdims=False)

    before = lax.ppermute(q_in[tokens - 2 :], "seq", [(i, i + 1) for i in range(seq - 1)])
    q = jnp.concatenate((before, q_in), axis=0).astype(F32)
    q_conv = short_filters[0, 0] * q[2:]
    for lag in (1, 2):
        q_conv = q_conv + short_filters[0, lag] * q[2 - lag : 2 - lag + tokens]
    q_conv_t = q_conv.T

    mine = lax.dynamic_slice_in_dim(short_filters, CH * lax.axis_index("seq"), CH, axis=2)
    h_strip = strips(long_filter.reshape(CH, B, B), "filter_strips")
    y, gated = long_conv(mine.reshape(-1), kv.reshape(2 * CH * seq, tokens), h_strip)
    both = project(homes, out_weight, (out_grad, r1, r2, r3, r4), q_conv_t, y)
    back = exchange(both.reshape(seq, 2 * CH, tokens), "seq")
    z_strip = strips(gated, "gated_strips")
    operator_out, filter_grad = grad_conv(back.reshape(2 * CH * seq, tokens), q_conv_t, z_strip)
    return operator_out, filter_grad.reshape(1, CH, B * B)


def solution(mesh):
    in_specs = (
        P("seq", "chan"),
        P("seq", "chan"),
        P("seq", "chan"),
        P(None, None, "chan"),
        P("chan", "seq", None),
        P("chan", None),
        P("seq", "chan"),
    )
    out_specs = (P("seq", "chan"), P("chan", "seq", None))
    return jax.shard_map(
        on_device, mesh=mesh, in_specs=in_specs, out_specs=out_specs, check_vma=False
    )
```

```python
import jax
import jax.numpy as jnp
from jax import lax
from jax.experimental import pallas as pl
from jax.experimental.pallas import tpu as pltpu
import ml_dtypes
import numpy as np
from jax.sharding import PartitionSpec as P

F32 = jnp.float32
BF16 = jnp.bfloat16
B = 128
PAIR = 2 * B
CH = 4
NT = (((1,), (1,)), ((), ()))


def iota2(shape, dim):
    return lax.broadcasted_iota(jnp.int32, shape, dim)


def spread_kernel(k_ref, v_ref, o_ref):
    row, col = iota2((PAIR, PAIR), 0), iota2((PAIR, PAIR), 1)
    source = (row // CH) % 2 * B + row // (2 * CH) * CH + row % CH
    pick = (col == source).astype(BF16)
    for g in range(4):
        lanes = slice(B * g, B * g + B)
        both = jnp.concatenate((k_ref[:, lanes], v_ref[:, lanes]), axis=1)
        rows = lax.dot_general(pick, both, NT, preferred_element_type=F32)
        o_ref[PAIR * g : PAIR * g + PAIR, :] = rows.astype(BF16)


def spread(k, v):
    return pl.pallas_call(
        spread_kernel, out_shape=jax.ShapeDtypeStruct((8 * B, B), BF16), name="spread"
    )(k, v)


def tables():
    def halves(x):
        high = x.astype(np.float32).astype(ml_dtypes.bfloat16)
        return high, (x - high.astype(np.float64)).astype(np.float32).astype(ml_dtypes.bfloat16)

    n = np.arange(B, dtype=np.float64)
    coarse = 2 * np.pi * (n[:, None] + 0.25) * n[None, :] / B
    turn = 2 * np.pi * (n[:, None] + 0.25) * n[None, :] / (B * B)
    fine = 2 * np.pi * (n[:, None] * n[None, :] % B) / B
    first = np.concatenate((np.cos(coarse), -np.sin(coarse)), 0)
    high, low = halves(first)
    into = np.concatenate((high, low), 1)
    high, low = halves(first.T / (B * B))
    out_of = np.concatenate((high, high, low), 1)
    cos, sin = np.cos(fine), np.sin(fine)
    high, low = halves(np.block([[cos, -sin], [sin, cos]]))
    down = np.concatenate((high, high, low), 0)
    high, low = halves(np.block([[cos, sin], [-sin, cos]]))
    up = np.concatenate((high, high, low), 0)
    twist = np.concatenate((np.cos(turn), -np.sin(turn)), 1).astype(np.float32)
    return into, down, up, out_of, twist


def split(x):
    high = x.astype(BF16)
    return high, (x - high.astype(F32)).astype(BF16)


def dot(x, y):
    return jnp.dot(x, y, preferred_element_type=F32)


def spectrum(high, low, into_ref, down_ref, twist_ref):
    first = dot(into_ref[...], jnp.concatenate((high, high), axis=0))
    if low is not None:
        first = first + dot(into_ref[:, 0:B], low)
    re, im = first[0:B, :], first[B:PAIR, :]
    cos, sin = twist_ref[:, 0:B], twist_ref[:, B:PAIR]
    turned = jnp.concatenate((re * cos - im * sin, re * sin + im * cos), axis=1)
    high, low = split(turned)
    return dot(jnp.concatenate((high, low, high), axis=1), down_ref[...])


def sequence(spec, up_ref, out_of_ref, twist_ref):
    high, low = split(spec)
    back = dot(jnp.concatenate((high, low, high), axis=1), up_ref[...])
    re, im = back[:, 0:B], back[:, B:PAIR]
    cos, sin = twist_ref[:, 0:B], twist_ref[:, B:PAIR]
    turned = jnp.concatenate((re * cos + im * sin, im * cos - re * sin), axis=0)
    high, low = split(turned)
    return dot(out_of_ref[...], jnp.concatenate((high, low, high), axis=0))


def filter_kernel(h_ref, into_ref, down_ref, twist_ref, o_ref):
    for c in range(CH):
        high, low = split(h_ref[pl.ds(c, B, stride=CH), :])
        o_ref[c] = spectrum(high, low, into_ref, down_ref, twist_ref)


def call(kernel, out_shape, name, flops, scratch_shapes=(), smem=0, inputs=0):
    vmem = pl.BlockSpec(memory_space=pltpu.VMEM)
    return pl.pallas_call(
        kernel,
        in_specs=[pl.BlockSpec(memory_space=pltpu.SMEM)] * smem + [vmem] * inputs,
        out_specs=jax.tree.map(lambda _: vmem, out_shape),
        out_shape=out_shape,
        scratch_shapes=scratch_shapes,
        compiler_params=pltpu.CompilerParams(vmem_limit_bytes=16 << 20),
        cost_estimate=pl.CostEstimate(flops=flops, transcendentals=0, bytes_accessed=2**21),
        name=name,
    )


SPECTRA = jax.ShapeDtypeStruct((CH, B, PAIR), F32)


def filter_spectra(h, into, down, twist):
    return call(filter_kernel, SPECTRA, "filter_spectra", 10**9, inputs=4)(h, into, down, twist)


def long_kernel(
    w_ref, kv_ref, h_ref, into_ref, down_ref, up_ref, out_of_ref, twist_ref, y_ref, z_ref, kvf, yf
):
    kvf[...] = kv_ref[...].astype(F32)
    row, lane = iota2((B, B), 0), iota2((B, B), 1)

    def short(stream, c):
        x = kvf[pl.ds(CH * stream + c, B, stride=2 * CH), :]
        before = jnp.where(row == 0, 0.0, pltpu.roll(x, 1, 0))
        out = w_ref[(stream + 1) * 12 + c] * x
        for lag in (1, 2):
            moved = pltpu.roll(jnp.where(lane < B - lag, x, before), lag, 1)
            out = out + w_ref[(stream + 1) * 12 + CH * lag + c] * moved
        return out

    for c in range(CH):
        gated = (short(0, c) * short(1, c)).astype(BF16)
        spec = spectrum(gated, None, into_ref, down_ref, twist_ref)
        z_ref[c] = spec
        re, im = spec[:, 0:B], spec[:, B:PAIR]
        hre, him = h_ref[c, :, 0:B], h_ref[c, :, B:PAIR]
        product = jnp.concatenate((re * hre - im * him, re * him + im * hre), axis=1)
        yf[pl.ds(c, B, stride=CH), :] = sequence(product, up_ref, out_of_ref, twist_ref)
    y_ref[...] = yf[...].astype(BF16)


def long_conv(w, kv, spectra, constants):
    into, down, up, out_of, twist = constants
    out_shape = [jax.ShapeDtypeStruct((CH * B, B), BF16), SPECTRA]
    scratch = [pltpu.VMEM((8 * B, B), F32), pltpu.VMEM((CH * B, B), F32)]
    return call(long_kernel, out_shape, "long_conv", 3 * 10**9, scratch, smem=1, inputs=7)(
        w, kv, spectra, into, down, up, out_of, twist
    )


def grad_kernel(
    back_ref, q_ref, z_ref, into_ref, down_ref, up_ref, out_of_ref, twist_ref, o_ref, f_ref, backf, yf
):
    backf[...] = back_ref[...].astype(F32)
    for c in range(CH):
        yf[pl.ds(c, B, stride=CH), :] = backf[pl.ds(c, B, stride=2 * CH), :]
        dy = backf[pl.ds(CH + c, B, stride=2 * CH), :].astype(BF16)
        spec = spectrum(dy, None, into_ref, down_ref, twist_ref)
        re, im = spec[:, 0:B], spec[:, B:PAIR]
        zre, zim = z_ref[c, :, 0:B], z_ref[c, :, B:PAIR]
        product = jnp.concatenate((re * zre + im * zim, im * zre - re * zim), axis=1)
        f_ref[pl.ds(c, B, stride=CH), :] = sequence(product, up_ref, out_of_ref, twist_ref)
    for g in range(CH):
        part = slice(B * g, B * g + B)
        o_ref[:, part] = (yf[part, :] * q_ref[part, :]).T.astype(BF16)


def grad_conv(back, q_conv_t, spectra, constants):
    into, down, up, out_of, twist = constants
    out_shape = [
        jax.ShapeDtypeStruct((B, CH * B), BF16),
        jax.ShapeDtypeStruct((CH * B, B), F32),
    ]
    scratch = [pltpu.VMEM((8 * B, B), F32), pltpu.VMEM((CH * B, B), F32)]
    return call(grad_kernel, out_shape, "grad_conv", 3 * 10**9, scratch, inputs=8)(
        back, q_conv_t, spectra, into, down, up, out_of, twist
    )


def project_kernel(at_ref, w_ref, a_ref, b_ref, c_ref, d_ref, e_ref, q_ref, y_ref, o_ref, df, yf, of):
    width = a_ref.shape[1]
    tokens = a_ref.shape[0]
    total = None
    blocks = [a_ref[...], b_ref[...]]
    for ref in (c_ref, d_ref, e_ref):
        blocks += [ref[0:tokens, :], ref[tokens : 2 * tokens, :]]
    for k, block in enumerate(blocks):
        start = pl.multiple_of(at_ref[k] * width, B)
        part = lax.dot_general(w_ref[:, pl.ds(start, width)], block, NT, preferred_element_type=F32)
        total = part if total is None else total + part
    df[...] = total * q_ref[...]
    yf[...] = y_ref[...].astype(F32)
    for c in range(CH):
        of[pl.ds(c, B, stride=2 * CH), :] = yf[pl.ds(c, B, stride=CH), :]
        of[pl.ds(CH + c, B, stride=2 * CH), :] = df[pl.ds(c, B, stride=CH), :]
    o_ref[...] = of[...].astype(BF16)


def project(order, weight, blocks, q_conv_t, y):
    vmem = pl.BlockSpec(memory_space=pltpu.VMEM)
    return pl.pallas_call(
        project_kernel,
        in_specs=[pl.BlockSpec(memory_space=pltpu.SMEM)] + [vmem] * 8,
        out_specs=vmem,
        out_shape=jax.ShapeDtypeStruct((8 * B, B), BF16),
        scratch_shapes=[
            pltpu.VMEM((CH * B, B), F32),
            pltpu.VMEM((CH * B, B), F32),
            pltpu.VMEM((8 * B, B), F32),
        ],
        compiler_params=pltpu.CompilerParams(vmem_limit_bytes=16 << 20),
        cost_estimate=pl.CostEstimate(flops=10**9, transcendentals=0, bytes_accessed=5 * 2**20),
        name="project",
    )(order, weight, *blocks, q_conv_t, y)


INNER = [(i, i ^ 1) for i in range(8)]
OUTER = [(i, (i + 1 if i % 2 else i - 1) % 8) for i in range(8)]


def swap_order():
    own = [[i] for i in range(8)]
    first = [own[i ^ 1] for i in range(8)]
    second = [own[j] + first[j] for _, j in OUTER]
    third = [second[j] for _, j in INNER]
    fourth = [third[j] for _, j in OUTER]
    return [sum(parts, []) for parts in zip(own, first, second, third, fourth, strict=True)]


def exchange(value, axis):
    return lax.all_to_all(value, axis, split_axis=0, concat_axis=0, tiled=True)


def on_device(q_in, k_in, v_in, short_filters, long_filter, out_weight, out_grad):
    tokens, width = q_in.shape
    seq = lax.axis_size("seq")
    z = lax.axis_index("chan")
    tie = lax.optimization_barrier
    r1 = lax.ppermute(out_grad, "chan", INNER)
    kv = spread(k_in, v_in)
    kv, r1 = tie((kv, r1))
    pair = jnp.concatenate((out_grad, r1), axis=0)
    r2 = lax.ppermute(pair, "chan", OUTER)
    kv = exchange(kv.reshape(seq, 2 * CH, tokens), "seq")
    r2, q_in, long_filter = tie((r2, q_in, long_filter))
    r3 = lax.ppermute(r2, "chan", INNER)
    r4 = lax.ppermute(r3, "chan", OUTER)
    homes = lax.dynamic_index_in_dim(jnp.array(swap_order(), jnp.int32), z, 0, keepdims=False)

    before = lax.ppermute(q_in[tokens - 2 :], "seq", [(i, i + 1) for i in range(seq - 1)])
    q = jnp.concatenate((before, q_in), axis=0).astype(F32)
    q_conv = short_filters[0, 0] * q[2:]
    for lag in (1, 2):
        q_conv = q_conv + short_filters[0, lag] * q[2 - lag : 2 - lag + tokens]
    q_conv_t = q_conv.T

    constants = [jnp.asarray(table) for table in tables()]
    into, down, _, _, twist = constants
    mine = lax.dynamic_slice_in_dim(short_filters, CH * lax.axis_index("seq"), CH, axis=2)
    h = long_filter.reshape(CH, B, B).transpose(1, 0, 2).reshape(CH * B, B)
    h_spectra = filter_spectra(h, into, down, twist)
    kv = kv.reshape(2 * CH * seq, tokens)
    y, z_spectra = long_conv(mine.reshape(-1), kv, h_spectra, constants)
    both = project(homes, out_weight, (out_grad, r1, r2, r3, r4), q_conv_t, y)
    back = exchange(both.reshape(seq, 2 * CH, tokens), "seq").reshape(2 * CH * seq, tokens)
    operator_out, filter_grad = grad_conv(back, q_conv_t, z_spectra, constants)
    filter_grad = filter_grad.reshape(B, CH, B).transpose(1, 0, 2)
    return operator_out, filter_grad.reshape(1, CH, B * B)


def solution(mesh):
    in_specs = (
        P("seq", "chan"),
        P("seq", "chan"),
        P("seq", "chan"),
        P(None, None, "chan"),
        P("chan", "seq", None),
        P("chan", None),
        P("seq", "chan"),
    )
    out_specs = (P("seq", "chan"), P("chan", "seq", None))
    return jax.shard_map(
        on_device, mesh=mesh, in_specs=in_specs, out_specs=out_specs, check_vma=False
    )
```

```python
import jax
import jax.numpy as jnp
from jax import lax
from jax.experimental import pallas as pl
from jax.experimental.pallas import tpu as pltpu
import ml_dtypes
import numpy as np
from jax.sharding import PartitionSpec as P

F32 = jnp.float32
BF16 = jnp.bfloat16
B = 128
PAIR = 2 * B
CH = 4
TAIL = 16
NT = (((1,), (1,)), ((), ()))


def iota2(shape, dim):
    return lax.broadcasted_iota(jnp.int32, shape, dim)


def spread_kernel(k_ref, v_ref, q_ref, o_ref, tail_ref):
    tail_ref[...] = q_ref[...]
    row, col = iota2((PAIR, PAIR), 0), iota2((PAIR, PAIR), 1)
    source = (row // CH) % 2 * B + row // (2 * CH) * CH + row % CH
    pick = (col == source).astype(BF16)
    for g in range(4):
        lanes = slice(B * g, B * g + B)
        both = jnp.concatenate((k_ref[:, lanes], v_ref[:, lanes]), axis=1)
        rows = lax.dot_general(pick, both, NT, preferred_element_type=F32)
        o_ref[PAIR * g : PAIR * g + PAIR, :] = rows.astype(BF16)


def spread(k, v, q):
    tokens, width = k.shape
    whole = lambda *shape: pl.BlockSpec(shape, lambda i: (0, 0))
    return pl.pallas_call(
        spread_kernel,
        grid=(1,),
        in_specs=[
            whole(tokens, width),
            whole(tokens, width),
            pl.BlockSpec((TAIL, width), lambda i: (tokens // TAIL - 1, 0)),
        ],
        out_specs=[whole(2 * width, tokens), whole(TAIL, width)],
        out_shape=[
            jax.ShapeDtypeStruct((2 * width, tokens), BF16),
            jax.ShapeDtypeStruct((TAIL, width), BF16),
        ],
        cost_estimate=pl.CostEstimate(flops=10**9, transcendentals=0, bytes_accessed=2**20),
        name="spread",
    )(k, v, q)


def tables():
    def halves(x):
        high = x.astype(np.float32).astype(ml_dtypes.bfloat16)
        return high, (x - high.astype(np.float64)).astype(np.float32).astype(ml_dtypes.bfloat16)

    n = np.arange(B, dtype=np.float64)
    coarse = 2 * np.pi * (n[:, None] + 0.25) * n[None, :] / B
    turn = 2 * np.pi * (n[:, None] + 0.25) * n[None, :] / (B * B)
    fine = 2 * np.pi * (n[:, None] * n[None, :] % B) / B
    first = np.concatenate((np.cos(coarse), -np.sin(coarse)), 0)
    high, low = halves(first)
    into = np.concatenate((high, low), 1)
    high, low = halves(first.T / (B * B))
    out_of = np.concatenate((high, high, low), 1)
    cos, sin = np.cos(fine), np.sin(fine)
    high, low = halves(np.block([[cos, -sin], [sin, cos]]))
    down = np.concatenate((high, high, low), 0)
    high, low = halves(np.block([[cos, sin], [-sin, cos]]))
    up = np.concatenate((high, high, low), 0)
    twist = np.concatenate((np.cos(turn), -np.sin(turn)), 1).astype(np.float32)
    return into, down, up, out_of, twist


def split(x):
    high = x.astype(BF16)
    return high, (x - high.astype(F32)).astype(BF16)


def dot(x, y):
    return jnp.dot(x, y, preferred_element_type=F32)


def spectrum(first, into_refs, wide, spec_ref):
    down_ref, twist_ref = into_refs
    cos, sin = twist_ref[:, 0:B], twist_ref[:, B:PAIR]
    for c in range(CH):
        lanes, rows = slice(B * c, B * c + B), slice(B * c, B * c + B)
        re, im = first[0:B, lanes], first[B:PAIR, lanes]
        stage(wide, rows, re * cos - im * sin, re * sin + im * cos)
    spec_ref[...] = dot(wide[...], down_ref[...])


def stage(wide, rows, re, im):
    for at, part in ((0, re), (B, im)):
        high, low = split(part)
        wide[rows, at : at + B] = high
        wide[rows, PAIR + at : PAIR + at + B] = low
        wide[rows, 2 * PAIR + at : 2 * PAIR + at + B] = high


def sequence(wide, back, tall, up_ref, out_of_ref, twist_ref):
    back[...] = dot(wide[...], up_ref[...])
    cos, sin = twist_ref[:, 0:B], twist_ref[:, B:PAIR]
    for c in range(CH):
        rows, lanes = slice(B * c, B * c + B), slice(B * c, B * c + B)
        re, im = back[rows, 0:B], back[rows, B:PAIR]
        for at, part in ((0, re * cos + im * sin), (B, im * cos - re * sin)):
            high, low = split(part)
            tall[at : at + B, lanes] = high
            tall[PAIR + at : PAIR + at + B, lanes] = low
            tall[2 * PAIR + at : 2 * PAIR + at + B, lanes] = high
    return dot(out_of_ref[...], tall[...])


def filter_kernel(h_ref, into_ref, down_ref, twist_ref, o_ref, wide):
    parts = [split(h_ref[pl.ds(c, B, stride=CH), :]) for c in range(CH)]
    high = jnp.concatenate([p[0] for p in parts], axis=1)
    low = jnp.concatenate([p[1] for p in parts], axis=1)
    first = dot(into_ref[...], jnp.concatenate((high, high), axis=0)) + dot(into_ref[:, 0:B], low)
    spectrum(first, (down_ref, twist_ref), wide, o_ref)


WIDE = pltpu.VMEM((CH * B, 3 * PAIR), BF16)
TALL = pltpu.VMEM((3 * PAIR, CH * B), BF16)
BACK = pltpu.VMEM((CH * B, PAIR), F32)


def call(kernel, out_shape, name, flops, scratch_shapes=(), smem=0, inputs=0):
    vmem = pl.BlockSpec(memory_space=pltpu.VMEM)
    return pl.pallas_call(
        kernel,
        in_specs=[pl.BlockSpec(memory_space=pltpu.SMEM)] * smem + [vmem] * inputs,
        out_specs=jax.tree.map(lambda _: vmem, out_shape),
        out_shape=out_shape,
        scratch_shapes=scratch_shapes,
        compiler_params=pltpu.CompilerParams(vmem_limit_bytes=16 << 20),
        cost_estimate=pl.CostEstimate(flops=flops, transcendentals=0, bytes_accessed=2**21),
        name=name,
    )


SPECTRA = jax.ShapeDtypeStruct((CH * B, PAIR), F32)


def filter_spectra(h, into, down, twist):
    return call(filter_kernel, SPECTRA, "filter_spectra", 10**10, [WIDE], inputs=4)(
        h, into, down, twist
    )


def long_kernel(
    w_ref, kv_ref, h_ref, into_ref, down_ref, up_ref, out_of_ref, twist_ref, y_ref, z_ref, *scratch
):
    kvf, yf, wide, tall, back = scratch
    kvf[...] = kv_ref[...].astype(F32)
    row, lane = iota2((B, B), 0), iota2((B, B), 1)
    mine = CH * lax.axis_index("seq")

    def short(stream, c):
        x = kvf[pl.ds(CH * stream + c, B, stride=2 * CH), :]
        before = jnp.where(row == 0, 0.0, pltpu.roll(x, 1, 0))
        out = w_ref[stream + 1, 0, mine + c] * x
        for lag in (1, 2):
            moved = pltpu.roll(jnp.where(lane < B - lag, x, before), lag, 1)
            out = out + w_ref[stream + 1, lag, mine + c] * moved
        return out

    gated = [(short(0, c) * short(1, c)).astype(BF16) for c in range(CH)]
    gated = jnp.concatenate(gated, axis=1)
    first = dot(into_ref[...], jnp.concatenate((gated, gated), axis=0))
    spectrum(first, (down_ref, twist_ref), wide, z_ref)
    for c in range(CH):
        rows = slice(B * c, B * c + B)
        re, im = z_ref[rows, 0:B], z_ref[rows, B:PAIR]
        hre, him = h_ref[rows, 0:B], h_ref[rows, B:PAIR]
        stage(wide, rows, re * hre - im * him, re * him + im * hre)
    y = sequence(wide, back, tall, up_ref, out_of_ref, twist_ref)
    for c in range(CH):
        yf[pl.ds(c, B, stride=CH), :] = y[:, B * c : B * c + B]
    y_ref[...] = yf[...].astype(BF16)


def long_conv(w, kv, spectra, constants):
    into, down, up, out_of, twist = constants
    out_shape = [jax.ShapeDtypeStruct((CH * B, B), BF16), SPECTRA]
    scratch = [pltpu.VMEM((8 * B, B), F32), pltpu.VMEM((CH * B, B), F32), WIDE, TALL, BACK]
    return call(long_kernel, out_shape, "long_conv", 10**10, scratch, smem=1, inputs=7)(
        w, kv, spectra, into, down, up, out_of, twist
    )


def grad_kernel(
    back_ref, q_ref, z_ref, into_ref, down_ref, up_ref, out_of_ref, twist_ref, o_ref, f_ref, *scratch
):
    backf, yf, wide, tall, back = scratch
    backf[...] = back_ref[...].astype(F32)
    dy = [backf[pl.ds(CH + c, B, stride=2 * CH), :].astype(BF16) for c in range(CH)]
    dy = jnp.concatenate(dy, axis=1)
    first = dot(into_ref[...], jnp.concatenate((dy, dy), axis=0))
    spectrum(first, (down_ref, twist_ref), wide, back)
    for c in range(CH):
        rows = slice(B * c, B * c + B)
        re, im = back[rows, 0:B], back[rows, B:PAIR]
        zre, zim = z_ref[rows, 0:B], z_ref[rows, B:PAIR]
        stage(wide, rows, re * zre + im * zim, im * zre - re * zim)
    grad = sequence(wide, back, tall, up_ref, out_of_ref, twist_ref)
    for c in range(CH):
        f_ref[pl.ds(c, B, stride=CH), :] = grad[:, B * c : B * c + B]
    for c in range(CH):
        yf[pl.ds(c, B, stride=CH), :] = backf[pl.ds(c, B, stride=2 * CH), :]
    for g in range(CH):
        part = slice(B * g, B * g + B)
        o_ref[:, part] = (yf[part, :] * q_ref[part, :]).T.astype(BF16)


def grad_conv(back, q_conv_t, spectra, constants):
    into, down, up, out_of, twist = constants
    out_shape = [
        jax.ShapeDtypeStruct((B, CH * B), BF16),
        jax.ShapeDtypeStruct((CH * B, B), F32),
    ]
    scratch = [pltpu.VMEM((8 * B, B), F32), pltpu.VMEM((CH * B, B), F32), WIDE, TALL, BACK]
    return call(grad_kernel, out_shape, "grad_conv", 3 * 10**9, scratch, inputs=8)(
        back, q_conv_t, spectra, into, down, up, out_of, twist
    )


def query_kernel(w_ref, q_ref, tail_ref, o_ref, qf):
    tokens = q_ref.shape[0]
    qf[0:TAIL, :] = tail_ref[...].astype(F32)
    qf[TAIL : TAIL + tokens, :] = q_ref[...].astype(F32)
    out = w_ref[0, 0:1, :] * qf[TAIL : TAIL + tokens, :]
    for lag in (1, 2):
        out = out + w_ref[0, lag : lag + 1, :] * qf[TAIL - lag : TAIL - lag + tokens, :]
    for g in range(CH):
        part = slice(B * g, B * g + B)
        o_ref[part, :] = out[:, part].T


def query_conv(w, q, tail):
    tokens, width = q.shape
    out_shape = jax.ShapeDtypeStruct((width, tokens), F32)
    scratch = [pltpu.VMEM((TAIL + tokens, width), F32)]
    return call(query_kernel, out_shape, "query_conv", 10**10, scratch, inputs=3)(w, q, tail)


def project_kernel(w_ref, a_ref, b_ref, c_ref, d_ref, e_ref, q_ref, y_ref, o_ref, df, yf, of):
    tokens, width = a_ref.shape
    z = lax.axis_index("chan")
    side = 1 - 2 * lax.rem(z, 2)
    wrap = lambda device: lax.rem(device + 16, 8)
    homes = [z, z + side, z - side, z - 2 * side, z + 2 * side, z + 3 * side, z - 3 * side, z - 4 * side]
    blocks = [a_ref[...], b_ref[...]]
    for ref in (c_ref, d_ref, e_ref):
        blocks += [ref[0:tokens, :], ref[tokens : 2 * tokens, :]]
    total = None
    for home, block in zip(homes, blocks, strict=True):
        start = pl.multiple_of(wrap(home) * width, B)
        part = lax.dot_general(w_ref[:, pl.ds(start, width)], block, NT, preferred_element_type=F32)
        total = part if total is None else total + part
    df[...] = total * q_ref[...]
    yf[...] = y_ref[...].astype(F32)
    for c in range(CH):
        of[pl.ds(c, B, stride=2 * CH), :] = yf[pl.ds(c, B, stride=CH), :]
        of[pl.ds(CH + c, B, stride=2 * CH), :] = df[pl.ds(c, B, stride=CH), :]
    o_ref[...] = of[...].astype(BF16)


def project(weight, blocks, q_conv_t, y):
    out_shape = jax.ShapeDtypeStruct((8 * B, B), BF16)
    scratch = [pltpu.VMEM((rows * B, B), F32) for rows in (CH, CH, 2 * CH)]
    return call(project_kernel, out_shape, "project", 10**9, scratch, inputs=8)(
        weight, *blocks, q_conv_t, y
    )


def exchange(value, axis):
    return lax.all_to_all(value, axis, split_axis=0, concat_axis=0, tiled=True)


INNER = [(i, i ^ 1) for i in range(8)]
OUTER = [(i, (i + 1 if i % 2 else i - 1) % 8) for i in range(8)]
SECOND = [(i, (i + 2 if i % 2 else i - 2) % 8) for i in range(8)]


def on_device(q_in, k_in, v_in, short_filters, long_filter, out_weight, out_grad):
    tokens, width = q_in.shape
    seq = lax.axis_size("seq")
    tie = lax.optimization_barrier

    r1 = lax.ppermute(out_grad, "chan", INNER)
    kv, tail = spread(k_in, v_in, q_in)
    kv, r1 = tie((kv, r1))
    pair = jnp.concatenate((out_grad, r1), axis=0)
    r2 = lax.ppermute(pair, "chan", OUTER)
    r3 = lax.ppermute(pair, "chan", SECOND)
    kv = exchange(kv.reshape(seq, 2 * CH, tokens), "seq")
    r2, r3, kv = tie((r2, r3, kv))
    r4 = lax.ppermute(r3, "chan", OUTER)
    before = lax.ppermute(tail, "seq", [(i, i + 1) for i in range(seq - 1)])

    constants = [jnp.asarray(table) for table in tables()]
    into, down, _, _, twist = constants
    h = long_filter.reshape(CH, B, B).transpose(1, 0, 2).reshape(CH * B, B)
    h_spectra = filter_spectra(h, into, down, twist)
    kv = kv.reshape(2 * CH * seq, tokens)
    y, z_spectra = long_conv(short_filters, kv, h_spectra, constants)
    q_conv_t = query_conv(short_filters, q_in, before)
    both = project(out_weight, (out_grad, r1, r2, r3, r4), q_conv_t, y)
    back = exchange(both.reshape(seq, 2 * CH, tokens), "seq").reshape(2 * CH * seq, tokens)
    operator_out, filter_grad = grad_conv(back, q_conv_t, z_spectra, constants)
    filter_grad = filter_grad.reshape(B, CH, B).transpose(1, 0, 2)
    return operator_out, filter_grad.reshape(1, CH, B * B)


def solution(mesh):
    in_specs = (
        P("seq", "chan"),
        P("seq", "chan"),
        P("seq", "chan"),
        P(None, None, "chan"),
        P("chan", "seq", None),
        P("chan", None),
        P("seq", "chan"),
    )
    out_specs = (P("seq", "chan"), P("chan", "seq", None))
    return jax.shard_map(
        on_device, mesh=mesh, in_specs=in_specs, out_specs=out_specs, check_vma=False
    )
```

```python
import jax
import jax.numpy as jnp
from jax import lax
from jax.experimental import pallas as pl
from jax.experimental.pallas import tpu as pltpu
import ml_dtypes
import numpy as np
from jax.sharding import PartitionSpec as P

F32 = jnp.float32
BF16 = jnp.bfloat16
B = 128
PAIR = 2 * B
CH = 4
TAIL = 16
NT = (((1,), (1,)), ((), ()))


def iota2(shape, dim):
    return lax.broadcasted_iota(jnp.int32, shape, dim)


def spread_kernel(k_ref, v_ref, q_ref, o_ref, tail_ref):
    tail_ref[...] = q_ref[...]
    row, col = iota2((PAIR, PAIR), 0), iota2((PAIR, PAIR), 1)
    source = (row // CH) % 2 * B + row // (2 * CH) * CH + row % CH
    pick = (col == source).astype(BF16)
    for g in range(4):
        lanes = slice(B * g, B * g + B)
        both = jnp.concatenate((k_ref[:, lanes], v_ref[:, lanes]), axis=1)
        rows = lax.dot_general(pick, both, NT, preferred_element_type=F32)
        o_ref[PAIR * g : PAIR * g + PAIR, :] = rows.astype(BF16)


def spread(k, v, q):
    tokens, width = k.shape
    whole = lambda *shape: pl.BlockSpec(shape, lambda i: (0, 0))
    return pl.pallas_call(
        spread_kernel,
        grid=(1,),
        in_specs=[
            whole(tokens, width),
            whole(tokens, width),
            pl.BlockSpec((TAIL, width), lambda i: (tokens // TAIL - 1, 0)),
        ],
        out_specs=[whole(2 * width, tokens), whole(TAIL, width)],
        out_shape=[
            jax.ShapeDtypeStruct((2 * width, tokens), BF16),
            jax.ShapeDtypeStruct((TAIL, width), BF16),
        ],
        cost_estimate=pl.CostEstimate(flops=10**9, transcendentals=0, bytes_accessed=2**20),
        name="spread",
    )(k, v, q)


def tables():
    def halves(x):
        high = x.astype(np.float32).astype(ml_dtypes.bfloat16)
        return high, (x - high.astype(np.float64)).astype(np.float32).astype(ml_dtypes.bfloat16)

    n = np.arange(B, dtype=np.float64)
    coarse = 2 * np.pi * (n[:, None] + 0.25) * n[None, :] / B
    turn = 2 * np.pi * (n[:, None] + 0.25) * n[None, :] / (B * B)
    fine = 2 * np.pi * (n[:, None] * n[None, :] % B) / B
    first = np.concatenate((np.cos(coarse), -np.sin(coarse)), 0)
    high, low = halves(first)
    into = np.concatenate((high, low), 1)
    high, low = halves(first.T / (B * B))
    out_of = np.concatenate((high, high, low), 1)
    cos, sin = np.cos(fine), np.sin(fine)
    high, low = halves(np.block([[cos, -sin], [sin, cos]]))
    down = np.concatenate((high, high, low), 0)
    high, low = halves(np.block([[cos, sin], [-sin, cos]]))
    up = np.concatenate((high, high, low), 0)
    twist = np.concatenate((np.cos(turn), -np.sin(turn)), 1).astype(np.float32)
    return into, down, up, out_of, twist


def split(x):
    high = x.astype(BF16)
    return high, (x - high.astype(F32)).astype(BF16)


def dot(x, y):
    return jnp.dot(x, y, preferred_element_type=F32)


def spectrum(first, into_refs, wide, spec_ref):
    down_ref, twist_ref = into_refs
    cos, sin = twist_ref[:, 0:B], twist_ref[:, B:PAIR]
    for c in range(CH):
        lanes, rows = slice(B * c, B * c + B), slice(B * c, B * c + B)
        re, im = first[0:B, lanes], first[B:PAIR, lanes]
        stage(wide, rows, re * cos - im * sin, re * sin + im * cos)
    spec_ref[...] = dot(wide[...], down_ref[...])


def stage(wide, rows, re, im):
    for at, part in ((0, re), (B, im)):
        high, low = split(part)
        wide[rows, at : at + B] = high
        wide[rows, PAIR + at : PAIR + at + B] = low
        wide[rows, 2 * PAIR + at : 2 * PAIR + at + B] = high


def sequence(wide, back, tall, up_ref, out_of_ref, twist_ref):
    back[...] = dot(wide[...], up_ref[...])
    cos, sin = twist_ref[:, 0:B], twist_ref[:, B:PAIR]
    for c in range(CH):
        rows, lanes = slice(B * c, B * c + B), slice(B * c, B * c + B)
        re, im = back[rows, 0:B], back[rows, B:PAIR]
        for at, part in ((0, re * cos + im * sin), (B, im * cos - re * sin)):
            high, low = split(part)
            tall[at : at + B, lanes] = high
            tall[PAIR + at : PAIR + at + B, lanes] = low
            tall[2 * PAIR + at : 2 * PAIR + at + B, lanes] = high
    return dot(out_of_ref[...], tall[...])


def filter_kernel(h_ref, into_ref, down_ref, twist_ref, o_ref, wide):
    parts = [split(h_ref[pl.ds(c, B, stride=CH), :]) for c in range(CH)]
    high = jnp.concatenate([p[0] for p in parts], axis=1)
    low = jnp.concatenate([p[1] for p in parts], axis=1)
    first = dot(into_ref[...], jnp.concatenate((high, high), axis=0)) + dot(into_ref[:, 0:B], low)
    spectrum(first, (down_ref, twist_ref), wide, o_ref)


WIDE = pltpu.VMEM((CH * B, 3 * PAIR), BF16)
TALL = pltpu.VMEM((3 * PAIR, CH * B), BF16)
BACK = pltpu.VMEM((CH * B, PAIR), F32)


def call(kernel, out_shape, name, flops, scratch_shapes=(), smem=0, inputs=0):
    vmem = pl.BlockSpec(memory_space=pltpu.VMEM)
    return pl.pallas_call(
        kernel,
        in_specs=[pl.BlockSpec(memory_space=pltpu.SMEM)] * smem + [vmem] * inputs,
        out_specs=jax.tree.map(lambda _: vmem, out_shape),
        out_shape=out_shape,
        scratch_shapes=scratch_shapes,
        compiler_params=pltpu.CompilerParams(vmem_limit_bytes=16 << 20),
        cost_estimate=pl.CostEstimate(flops=flops, transcendentals=0, bytes_accessed=2**21),
        name=name,
    )


SPECTRA = jax.ShapeDtypeStruct((CH * B, PAIR), F32)


def filter_spectra(h, into, down, twist):
    return call(filter_kernel, SPECTRA, "filter_spectra", 10**10, [WIDE], inputs=4)(
        h, into, down, twist
    )


def long_kernel(
    w_ref, kv_ref, h_ref, into_ref, down_ref, up_ref, out_of_ref, twist_ref, y_ref, z_ref, *scratch
):
    kvf, yf, wide, tall, back = scratch
    kvf[...] = kv_ref[...].astype(F32)
    row, lane = iota2((B, B), 0), iota2((B, B), 1)
    mine = CH * lax.axis_index("seq")

    def short(stream, c):
        x = kvf[pl.ds(CH * stream + c, B, stride=2 * CH), :]
        before = jnp.where(row == 0, 0.0, pltpu.roll(x, 1, 0))
        out = w_ref[stream + 1, 0, mine + c] * x
        for lag in (1, 2):
            moved = pltpu.roll(jnp.where(lane < B - lag, x, before), lag, 1)
            out = out + w_ref[stream + 1, lag, mine + c] * moved
        return out

    gated = [(short(0, c) * short(1, c)).astype(BF16) for c in range(CH)]
    gated = jnp.concatenate(gated, axis=1)
    first = dot(into_ref[...], jnp.concatenate((gated, gated), axis=0))
    spectrum(first, (down_ref, twist_ref), wide, z_ref)
    for c in range(CH):
        rows = slice(B * c, B * c + B)
        re, im = z_ref[rows, 0:B], z_ref[rows, B:PAIR]
        hre, him = h_ref[rows, 0:B], h_ref[rows, B:PAIR]
        stage(wide, rows, re * hre - im * him, re * him + im * hre)
    y = sequence(wide, back, tall, up_ref, out_of_ref, twist_ref)
    for c in range(CH):
        yf[pl.ds(c, B, stride=CH), :] = y[:, B * c : B * c + B]
    y_ref[...] = yf[...].astype(BF16)


def long_conv(w, kv, spectra, constants):
    into, down, up, out_of, twist = constants
    out_shape = [jax.ShapeDtypeStruct((CH * B, B), BF16), SPECTRA]
    scratch = [pltpu.VMEM((8 * B, B), F32), pltpu.VMEM((CH * B, B), F32), WIDE, TALL, BACK]
    return call(long_kernel, out_shape, "long_conv", 10**10, scratch, smem=1, inputs=7)(
        w, kv, spectra, into, down, up, out_of, twist
    )


def grad_kernel(
    back_ref, q_ref, z_ref, into_ref, down_ref, up_ref, out_of_ref, twist_ref, o_ref, f_ref, *scratch
):
    backf, yf, wide, tall, back = scratch
    backf[...] = back_ref[...].astype(F32)
    dy = [backf[pl.ds(CH + c, B, stride=2 * CH), :].astype(BF16) for c in range(CH)]
    dy = jnp.concatenate(dy, axis=1)
    first = dot(into_ref[...], jnp.concatenate((dy, dy), axis=0))
    spectrum(first, (down_ref, twist_ref), wide, back)
    for c in range(CH):
        rows = slice(B * c, B * c + B)
        re, im = back[rows, 0:B], back[rows, B:PAIR]
        zre, zim = z_ref[rows, 0:B], z_ref[rows, B:PAIR]
        stage(wide, rows, re * zre + im * zim, im * zre - re * zim)
    grad = sequence(wide, back, tall, up_ref, out_of_ref, twist_ref)
    for c in range(CH):
        f_ref[pl.ds(c, B, stride=CH), :] = grad[:, B * c : B * c + B]
    for c in range(CH):
        yf[pl.ds(c, B, stride=CH), :] = backf[pl.ds(c, B, stride=2 * CH), :]
    for g in range(CH):
        part = slice(B * g, B * g + B)
        o_ref[:, part] = (yf[part, :] * q_ref[part, :]).T.astype(BF16)


def grad_conv(back, q_conv_t, spectra, constants):
    into, down, up, out_of, twist = constants
    out_shape = [
        jax.ShapeDtypeStruct((B, CH * B), BF16),
        jax.ShapeDtypeStruct((CH * B, B), F32),
    ]
    scratch = [pltpu.VMEM((8 * B, B), F32), pltpu.VMEM((CH * B, B), F32), WIDE, TALL, BACK]
    return call(grad_kernel, out_shape, "grad_conv", 3 * 10**9, scratch, inputs=8)(
        back, q_conv_t, spectra, into, down, up, out_of, twist
    )


def query_kernel(w_ref, q_ref, tail_ref, o_ref, qf):
    tokens = q_ref.shape[0]
    qf[0:TAIL, :] = tail_ref[...].astype(F32)
    qf[TAIL : TAIL + tokens, :] = q_ref[...].astype(F32)
    out = w_ref[0, 0:1, :] * qf[TAIL : TAIL + tokens, :]
    for lag in (1, 2):
        out = out + w_ref[0, lag : lag + 1, :] * qf[TAIL - lag : TAIL - lag + tokens, :]
    for g in range(CH):
        part = slice(B * g, B * g + B)
        o_ref[part, :] = out[:, part].T


def query_conv(w, q, tail):
    tokens, width = q.shape
    out_shape = jax.ShapeDtypeStruct((width, tokens), F32)
    scratch = [pltpu.VMEM((TAIL + tokens, width), F32)]
    return call(query_kernel, out_shape, "query_conv", 10**10, scratch, inputs=3)(w, q, tail)


def project_kernel(w_ref, a_ref, b_ref, c_ref, d_ref, e_ref, q_ref, y_ref, o_ref, df, yf, of):
    tokens, width = a_ref.shape
    z = lax.axis_index("chan")
    side = 1 - 2 * lax.rem(z, 2)
    wrap = lambda device: lax.rem(device + 16, 8)
    homes = [z, z + side, z - side, z - 2 * side, z + 2 * side, z + 3 * side, z - 3 * side, z - 4 * side]
    blocks = [a_ref[...], b_ref[...]]
    for ref in (c_ref, d_ref, e_ref):
        blocks += [ref[0:tokens, :], ref[tokens : 2 * tokens, :]]
    total = None
    for home, block in zip(homes, blocks, strict=True):
        start = pl.multiple_of(wrap(home) * width, B)
        part = lax.dot_general(w_ref[:, pl.ds(start, width)], block, NT, preferred_element_type=F32)
        total = part if total is None else total + part
    df[...] = total * q_ref[...]
    yf[...] = y_ref[...].astype(F32)
    for c in range(CH):
        of[pl.ds(c, B, stride=2 * CH), :] = yf[pl.ds(c, B, stride=CH), :]
        of[pl.ds(CH + c, B, stride=2 * CH), :] = df[pl.ds(c, B, stride=CH), :]
    o_ref[...] = of[...].astype(BF16)


def project(weight, blocks, q_conv_t, y):
    out_shape = jax.ShapeDtypeStruct((8 * B, B), BF16)
    scratch = [pltpu.VMEM((rows * B, B), F32) for rows in (CH, CH, 2 * CH)]
    return call(project_kernel, out_shape, "project", 10**9, scratch, inputs=8)(
        weight, *blocks, q_conv_t, y
    )


def exchange(value, axis):
    return lax.all_to_all(value, axis, split_axis=0, concat_axis=0, tiled=True)


INNER = [(i, i ^ 1) for i in range(8)]
OUTER = [(i, (i + 1 if i % 2 else i - 1) % 8) for i in range(8)]
SECOND = [(i, (i + 2 if i % 2 else i - 2) % 8) for i in range(8)]


def on_device(q_in, k_in, v_in, short_filters, long_filter, out_weight, out_grad):
    tokens, width = q_in.shape
    seq = lax.axis_size("seq")
    tie = lax.optimization_barrier

    r1 = lax.ppermute(out_grad, "chan", INNER)
    kv, tail = spread(k_in, v_in, q_in)
    kv, r1 = tie((kv, r1))
    pair = jnp.concatenate((out_grad, r1), axis=0)
    r2 = lax.ppermute(pair, "chan", OUTER)
    r3 = lax.ppermute(pair, "chan", SECOND)
    kv = exchange(kv.reshape(seq, 2 * CH, tokens), "seq")
    r2, r3, tail, long_filter = tie((r2, r3, tail, long_filter))
    r4 = lax.ppermute(r3, "chan", OUTER)
    before = lax.ppermute(tail, "seq", [(i, i + 1) for i in range(seq - 1)])

    constants = [jnp.asarray(table) for table in tables()]
    into, down, _, _, twist = constants
    h = long_filter.reshape(CH, B, B).transpose(1, 0, 2).reshape(CH * B, B)
    h_spectra = filter_spectra(h, into, down, twist)
    kv = kv.reshape(2 * CH * seq, tokens)
    y, z_spectra = long_conv(short_filters, kv, h_spectra, constants)
    q_conv_t = query_conv(short_filters, q_in, before)
    both = project(out_weight, (out_grad, r1, r2, r3, r4), q_conv_t, y)
    back = exchange(both.reshape(seq, 2 * CH, tokens), "seq").reshape(2 * CH * seq, tokens)
    operator_out, filter_grad = grad_conv(back, q_conv_t, z_spectra, constants)
    filter_grad = filter_grad.reshape(B, CH, B).transpose(1, 0, 2)
    return operator_out, filter_grad.reshape(1, CH, B * B)


def solution(mesh):
    in_specs = (
        P("seq", "chan"),
        P("seq", "chan"),
        P("seq", "chan"),
        P(None, None, "chan"),
        P("chan", "seq", None),
        P("chan", None),
        P("seq", "chan"),
    )
    out_specs = (P("seq", "chan"), P("chan", "seq", None))
    return jax.shard_map(
        on_device, mesh=mesh, in_specs=in_specs, out_specs=out_specs, check_vma=False
    )
```

```python
import jax
import jax.numpy as jnp
from jax import lax
from jax.experimental import pallas as pl
from jax.experimental.pallas import tpu as pltpu
import ml_dtypes
import numpy as np
from jax.sharding import PartitionSpec as P

F32 = jnp.float32
BF16 = jnp.bfloat16
B = 128
PAIR = 2 * B
CH = 4
TAIL = 16
NT = (((1,), (1,)), ((), ()))


def iota2(shape, dim):
    return lax.broadcasted_iota(jnp.int32, shape, dim)


def spread_kernel(k_ref, v_ref, q_ref, o_ref, tail_ref):
    tail_ref[...] = q_ref[...]
    row, col = iota2((PAIR, PAIR), 0), iota2((PAIR, PAIR), 1)
    source = (row // CH) % 2 * B + row // (2 * CH) * CH + row % CH
    pick = (col == source).astype(BF16)
    for g in range(4):
        lanes = slice(B * g, B * g + B)
        both = jnp.concatenate((k_ref[:, lanes], v_ref[:, lanes]), axis=1)
        rows = lax.dot_general(pick, both, NT, preferred_element_type=F32)
        o_ref[PAIR * g : PAIR * g + PAIR, :] = rows.astype(BF16)


def spread(k, v, q):
    tokens, width = k.shape
    whole = lambda *shape: pl.BlockSpec(shape, lambda i: (0, 0))
    return pl.pallas_call(
        spread_kernel,
        grid=(1,),
        in_specs=[
            whole(tokens, width),
            whole(tokens, width),
            pl.BlockSpec((TAIL, width), lambda i: (tokens // TAIL - 1, 0)),
        ],
        out_specs=[whole(2 * width, tokens), whole(TAIL, width)],
        out_shape=[
            jax.ShapeDtypeStruct((2 * width, tokens), BF16),
            jax.ShapeDtypeStruct((TAIL, width), BF16),
        ],
        cost_estimate=pl.CostEstimate(flops=10**9, transcendentals=0, bytes_accessed=2**20),
        name="spread",
    )(k, v, q)


def tables():
    def halves(x):
        high = x.astype(np.float32).astype(ml_dtypes.bfloat16)
        return high, (x - high.astype(np.float64)).astype(np.float32).astype(ml_dtypes.bfloat16)

    n = np.arange(B, dtype=np.float64)
    coarse = 2 * np.pi * (n[:, None] + 0.25) * n[None, :] / B
    turn = 2 * np.pi * (n[:, None] + 0.25) * n[None, :] / (B * B)
    fine = 2 * np.pi * (n[:, None] * n[None, :] % B) / B
    first = np.concatenate((np.cos(coarse), -np.sin(coarse)), 0)
    high, low = halves(first)
    into = np.concatenate((high, low), 1)
    high, low = halves(first.T / (B * B))
    out_of = np.concatenate((high, high, low), 1)
    cos, sin = np.cos(fine), np.sin(fine)
    high, low = halves(np.block([[cos, -sin], [sin, cos]]))
    down = np.concatenate((high, high, low), 0)
    high, low = halves(np.block([[cos, sin], [-sin, cos]]))
    up = np.concatenate((high, high, low), 0)
    twist = np.concatenate((np.cos(turn), -np.sin(turn)), 1).astype(np.float32)
    return into, down, up, out_of, twist


def split(x):
    high = x.astype(BF16)
    return high, (x - high.astype(F32)).astype(BF16)


def dot(x, y):
    return jnp.dot(x, y, preferred_element_type=F32)


def spectrum(first, into_refs, wide, spec_ref):
    down_ref, twist_ref = into_refs
    cos, sin = twist_ref[:, 0:B], twist_ref[:, B:PAIR]
    for c in range(CH):
        lanes, rows = slice(B * c, B * c + B), slice(B * c, B * c + B)
        re, im = first[0:B, lanes], first[B:PAIR, lanes]
        stage(wide, rows, re * cos - im * sin, re * sin + im * cos)
    spec_ref[...] = dot(wide[...], down_ref[...])


def stage(wide, rows, re, im):
    for at, part in ((0, re), (B, im)):
        high, low = split(part)
        wide[rows, at : at + B] = high
        wide[rows, PAIR + at : PAIR + at + B] = low
        wide[rows, 2 * PAIR + at : 2 * PAIR + at + B] = high


def sequence(wide, back, tall, up_ref, out_of_ref, twist_ref):
    back[...] = dot(wide[...], up_ref[...])
    cos, sin = twist_ref[:, 0:B], twist_ref[:, B:PAIR]
    for c in range(CH):
        rows, lanes = slice(B * c, B * c + B), slice(B * c, B * c + B)
        re, im = back[rows, 0:B], back[rows, B:PAIR]
        for at, part in ((0, re * cos + im * sin), (B, im * cos - re * sin)):
            high, low = split(part)
            tall[at : at + B, lanes] = high
            tall[PAIR + at : PAIR + at + B, lanes] = low
            tall[2 * PAIR + at : 2 * PAIR + at + B, lanes] = high
    return dot(out_of_ref[...], tall[...])


def filter_kernel(h_ref, into_ref, down_ref, twist_ref, o_ref, wide):
    parts = [split(h_ref[pl.ds(c, B, stride=CH), :]) for c in range(CH)]
    high = jnp.concatenate([p[0] for p in parts], axis=1)
    low = jnp.concatenate([p[1] for p in parts], axis=1)
    first = dot(into_ref[...], jnp.concatenate((high, high), axis=0)) + dot(into_ref[:, 0:B], low)
    spectrum(first, (down_ref, twist_ref), wide, o_ref)


WIDE = pltpu.VMEM((CH * B, 3 * PAIR), BF16)
TALL = pltpu.VMEM((3 * PAIR, CH * B), BF16)
BACK = pltpu.VMEM((CH * B, PAIR), F32)


def call(kernel, out_shape, name, flops, scratch_shapes=(), smem=0, inputs=0):
    vmem = pl.BlockSpec(memory_space=pltpu.VMEM)
    return pl.pallas_call(
        kernel,
        in_specs=[pl.BlockSpec(memory_space=pltpu.SMEM)] * smem + [vmem] * inputs,
        out_specs=jax.tree.map(lambda _: vmem, out_shape),
        out_shape=out_shape,
        scratch_shapes=scratch_shapes,
        compiler_params=pltpu.CompilerParams(vmem_limit_bytes=16 << 20),
        cost_estimate=pl.CostEstimate(flops=flops, transcendentals=0, bytes_accessed=2**21),
        name=name,
    )


SPECTRA = jax.ShapeDtypeStruct((CH * B, PAIR), F32)


def filter_spectra(h, into, down, twist):
    return call(filter_kernel, SPECTRA, "filter_spectra", 10**10, [WIDE], inputs=4)(
        h, into, down, twist
    )


def long_kernel(
    w_ref, kv_ref, h_ref, into_ref, down_ref, up_ref, out_of_ref, twist_ref, y_ref, z_ref, *scratch
):
    kvf, yf, wide, tall, back = scratch
    kvf[...] = kv_ref[...].astype(F32)
    row, lane = iota2((B, B), 0), iota2((B, B), 1)
    mine = CH * lax.axis_index("seq")

    def short(stream, c):
        x = kvf[pl.ds(CH * stream + c, B, stride=2 * CH), :]
        before = jnp.where(row == 0, 0.0, pltpu.roll(x, 1, 0))
        out = w_ref[stream + 1, 0, mine + c] * x
        for lag in (1, 2):
            moved = pltpu.roll(jnp.where(lane < B - lag, x, before), lag, 1)
            out = out + w_ref[stream + 1, lag, mine + c] * moved
        return out

    gated = [(short(0, c) * short(1, c)).astype(BF16) for c in range(CH)]
    gated = jnp.concatenate(gated, axis=1)
    first = dot(into_ref[...], jnp.concatenate((gated, gated), axis=0))
    spectrum(first, (down_ref, twist_ref), wide, z_ref)
    for c in range(CH):
        rows = slice(B * c, B * c + B)
        re, im = z_ref[rows, 0:B], z_ref[rows, B:PAIR]
        hre, him = h_ref[rows, 0:B], h_ref[rows, B:PAIR]
        stage(wide, rows, re * hre - im * him, re * him + im * hre)
    y = sequence(wide, back, tall, up_ref, out_of_ref, twist_ref)
    for c in range(CH):
        yf[pl.ds(c, B, stride=CH), :] = y[:, B * c : B * c + B]
    y_ref[...] = yf[...].astype(BF16)


def long_conv(w, kv, spectra, constants):
    into, down, up, out_of, twist = constants
    out_shape = [jax.ShapeDtypeStruct((CH * B, B), BF16), SPECTRA]
    scratch = [pltpu.VMEM((8 * B, B), F32), pltpu.VMEM((CH * B, B), F32), WIDE, TALL, BACK]
    return call(long_kernel, out_shape, "long_conv", 10**10, scratch, smem=1, inputs=7)(
        w, kv, spectra, into, down, up, out_of, twist
    )


def grad_kernel(
    back_ref, q_ref, z_ref, into_ref, down_ref, up_ref, out_of_ref, twist_ref, o_ref, f_ref, *scratch
):
    backf, yf, wide, tall, back = scratch
    backf[...] = back_ref[...].astype(F32)
    dy = [backf[pl.ds(CH + c, B, stride=2 * CH), :].astype(BF16) for c in range(CH)]
    dy = jnp.concatenate(dy, axis=1)
    first = dot(into_ref[...], jnp.concatenate((dy, dy), axis=0))
    spectrum(first, (down_ref, twist_ref), wide, back)
    for c in range(CH):
        rows = slice(B * c, B * c + B)
        re, im = back[rows, 0:B], back[rows, B:PAIR]
        zre, zim = z_ref[rows, 0:B], z_ref[rows, B:PAIR]
        stage(wide, rows, re * zre + im * zim, im * zre - re * zim)
    grad = sequence(wide, back, tall, up_ref, out_of_ref, twist_ref)
    for c in range(CH):
        f_ref[pl.ds(c, B, stride=CH), :] = grad[:, B * c : B * c + B]
    for c in range(CH):
        yf[pl.ds(c, B, stride=CH), :] = backf[pl.ds(c, B, stride=2 * CH), :]
    for g in range(CH):
        part = slice(B * g, B * g + B)
        o_ref[:, part] = (yf[part, :] * q_ref[part, :]).T.astype(BF16)


def grad_conv(back, q_conv_t, spectra, constants):
    into, down, up, out_of, twist = constants
    out_shape = [
        jax.ShapeDtypeStruct((B, CH * B), BF16),
        jax.ShapeDtypeStruct((CH * B, B), F32),
    ]
    scratch = [pltpu.VMEM((8 * B, B), F32), pltpu.VMEM((CH * B, B), F32), WIDE, TALL, BACK]
    return call(grad_kernel, out_shape, "grad_conv", 3 * 10**9, scratch, inputs=8)(
        back, q_conv_t, spectra, into, down, up, out_of, twist
    )


def query_kernel(w_ref, q_ref, tail_ref, o_ref, qf):
    tokens = q_ref.shape[0]
    qf[0:TAIL, :] = tail_ref[...].astype(F32)
    qf[TAIL : TAIL + tokens, :] = q_ref[...].astype(F32)
    out = w_ref[0, 0:1, :] * qf[TAIL : TAIL + tokens, :]
    for lag in (1, 2):
        out = out + w_ref[0, lag : lag + 1, :] * qf[TAIL - lag : TAIL - lag + tokens, :]
    for g in range(CH):
        part = slice(B * g, B * g + B)
        o_ref[part, :] = out[:, part].T


def query_conv(w, q, tail):
    tokens, width = q.shape
    out_shape = jax.ShapeDtypeStruct((width, tokens), F32)
    scratch = [pltpu.VMEM((TAIL + tokens, width), F32)]
    return call(query_kernel, out_shape, "query_conv", 10**10, scratch, inputs=3)(w, q, tail)


def project_kernel(w_ref, a_ref, b_ref, c_ref, d_ref, e_ref, q_ref, y_ref, o_ref, df, yf, of):
    tokens, width = a_ref.shape
    z = lax.axis_index("chan")
    side = 1 - 2 * lax.rem(z, 2)
    wrap = lambda device: lax.rem(device + 16, 8)
    homes = [z, z + side, z - side, z - 2 * side, z + 2 * side, z + 3 * side, z - 3 * side, z - 4 * side]
    blocks = [a_ref[...], b_ref[...]]
    for ref in (c_ref, d_ref, e_ref):
        blocks += [ref[0:tokens, :], ref[tokens : 2 * tokens, :]]
    total = None
    for home, block in zip(homes, blocks, strict=True):
        start = pl.multiple_of(wrap(home) * width, B)
        part = lax.dot_general(w_ref[:, pl.ds(start, width)], block, NT, preferred_element_type=F32)
        total = part if total is None else total + part
    df[...] = total * q_ref[...]
    yf[...] = y_ref[...].astype(F32)
    for c in range(CH):
        of[pl.ds(c, B, stride=2 * CH), :] = yf[pl.ds(c, B, stride=CH), :]
        of[pl.ds(CH + c, B, stride=2 * CH), :] = df[pl.ds(c, B, stride=CH), :]
    o_ref[...] = of[...].astype(BF16)


def project(weight, blocks, q_conv_t, y):
    out_shape = jax.ShapeDtypeStruct((8 * B, B), BF16)
    scratch = [pltpu.VMEM((rows * B, B), F32) for rows in (CH, CH, 2 * CH)]
    return call(project_kernel, out_shape, "project", 10**9, scratch, inputs=8)(
        weight, *blocks, q_conv_t, y
    )


def exchange(value, axis):
    return lax.all_to_all(value, axis, split_axis=0, concat_axis=0, tiled=True)


INNER = [(i, i ^ 1) for i in range(8)]
OUTER = [(i, (i + 1 if i % 2 else i - 1) % 8) for i in range(8)]
SECOND = [(i, (i + 2 if i % 2 else i - 2) % 8) for i in range(8)]


def on_device(q_in, k_in, v_in, short_filters, long_filter, out_weight, out_grad):
    tokens, width = q_in.shape
    seq = lax.axis_size("seq")
    tie = lax.optimization_barrier

    r1 = lax.ppermute(out_grad, "chan", INNER)
    kv, tail = spread(k_in, v_in, q_in)
    before = lax.ppermute(tail, "seq", [(i, i + 1) for i in range(seq - 1)])
    kv, r1, before = tie((kv, r1, before))
    pair = jnp.concatenate((out_grad, r1), axis=0)
    r2 = lax.ppermute(pair, "chan", OUTER)
    r3 = lax.ppermute(pair, "chan", SECOND)
    kv = exchange(kv.reshape(seq, 2 * CH, tokens), "seq")
    r2, r3, long_filter, before = tie((r2, r3, long_filter, before))
    r4 = lax.ppermute(r3, "chan", OUTER)

    constants = [jnp.asarray(table) for table in tables()]
    into, down, _, _, twist = constants
    h = long_filter.reshape(CH, B, B).transpose(1, 0, 2).reshape(CH * B, B)
    h_spectra = filter_spectra(h, into, down, twist)
    kv = kv.reshape(2 * CH * seq, tokens)
    y, z_spectra = long_conv(short_filters, kv, h_spectra, constants)
    q_conv_t = query_conv(short_filters, q_in, before)
    both = project(out_weight, (out_grad, r1, r2, r3, r4), q_conv_t, y)
    back = exchange(both.reshape(seq, 2 * CH, tokens), "seq").reshape(2 * CH * seq, tokens)
    operator_out, filter_grad = grad_conv(back, q_conv_t, z_spectra, constants)
    filter_grad = filter_grad.reshape(B, CH, B).transpose(1, 0, 2)
    return operator_out, filter_grad.reshape(1, CH, B * B)


def solution(mesh):
    in_specs = (
        P("seq", "chan"),
        P("seq", "chan"),
        P("seq", "chan"),
        P(None, None, "chan"),
        P("chan", "seq", None),
        P("chan", None),
        P("seq", "chan"),
    )
    out_specs = (P("seq", "chan"), P("chan", "seq", None))
    return jax.shard_map(
        on_device, mesh=mesh, in_specs=in_specs, out_specs=out_specs, check_vma=False
    )
```

```python
import jax
import jax.numpy as jnp
from jax import lax
from jax.experimental import pallas as pl
from jax.experimental.pallas import tpu as pltpu
import ml_dtypes
import numpy as np
from jax.sharding import PartitionSpec as P

F32 = jnp.float32
BF16 = jnp.bfloat16
B = 128
PAIR = 2 * B
CH = 4
TAIL = 16
NT = (((1,), (1,)), ((), ()))


def iota2(shape, dim):
    return lax.broadcasted_iota(jnp.int32, shape, dim)


def spread_kernel(k_ref, v_ref, q_ref, o_ref, tail_ref):
    tail_ref[...] = q_ref[...]
    row, col = iota2((PAIR, PAIR), 0), iota2((PAIR, PAIR), 1)
    source = (row // CH) % 2 * B + row // (2 * CH) * CH + row % CH
    pick = (col == source).astype(BF16)
    for g in range(4):
        lanes = slice(B * g, B * g + B)
        both = jnp.concatenate((k_ref[:, lanes], v_ref[:, lanes]), axis=1)
        rows = lax.dot_general(pick, both, NT, preferred_element_type=F32)
        o_ref[PAIR * g : PAIR * g + PAIR, :] = rows.astype(BF16)


def spread(k, v, q):
    tokens, width = k.shape
    whole = lambda *shape: pl.BlockSpec(shape, lambda i: (0, 0))
    return pl.pallas_call(
        spread_kernel,
        grid=(1,),
        in_specs=[
            whole(tokens, width),
            whole(tokens, width),
            pl.BlockSpec((TAIL, width), lambda i: (tokens // TAIL - 1, 0)),
        ],
        out_specs=[whole(2 * width, tokens), whole(TAIL, width)],
        out_shape=[
            jax.ShapeDtypeStruct((2 * width, tokens), BF16),
            jax.ShapeDtypeStruct((TAIL, width), BF16),
        ],
        cost_estimate=pl.CostEstimate(flops=10**9, transcendentals=0, bytes_accessed=2**20),
        name="spread",
    )(k, v, q)


def tables():
    def halves(x):
        high = x.astype(np.float32).astype(ml_dtypes.bfloat16)
        return high, (x - high.astype(np.float64)).astype(np.float32).astype(ml_dtypes.bfloat16)

    n = np.arange(B, dtype=np.float64)
    coarse = 2 * np.pi * (n[:, None] + 0.25) * n[None, :] / B
    turn = 2 * np.pi * (n[:, None] + 0.25) * n[None, :] / (B * B)
    fine = 2 * np.pi * (n[:, None] * n[None, :] % B) / B
    first = np.concatenate((np.cos(coarse), -np.sin(coarse)), 0)
    high, low = halves(first)
    into = np.concatenate((high, low), 1)
    high, low = halves(first.T / (B * B))
    out_of = np.concatenate((high, high, low), 1)
    cos, sin = np.cos(fine), np.sin(fine)
    high, low = halves(np.block([[cos, -sin], [sin, cos]]))
    down = np.concatenate((high, high, low), 0)
    high, low = halves(np.block([[cos, sin], [-sin, cos]]))
    up = np.concatenate((high, high, low), 0)
    twist = np.concatenate((np.cos(turn), -np.sin(turn)), 1).astype(np.float32)
    return into, down, up, out_of, twist


def split(x):
    high = x.astype(BF16)
    return high, (x - high.astype(F32)).astype(BF16)


def dot(x, y):
    return jnp.dot(x, y, preferred_element_type=F32)


def spectrum(first, into_refs, wide, spec_ref):
    down_ref, twist_ref = into_refs
    cos, sin = twist_ref[:, 0:B], twist_ref[:, B:PAIR]
    for c in range(CH):
        lanes, rows = slice(B * c, B * c + B), slice(B * c, B * c + B)
        re, im = first[0:B, lanes], first[B:PAIR, lanes]
        stage(wide, rows, re * cos - im * sin, re * sin + im * cos)
    spec_ref[...] = dot(wide[...], down_ref[...])


def stage(wide, rows, re, im):
    for at, part in ((0, re), (B, im)):
        high, low = split(part)
        wide[rows, at : at + B] = high
        wide[rows, PAIR + at : PAIR + at + B] = low
        wide[rows, 2 * PAIR + at : 2 * PAIR + at + B] = high


def sequence(wide, back, tall, up_ref, out_of_ref, twist_ref):
    back[...] = dot(wide[...], up_ref[...])
    cos, sin = twist_ref[:, 0:B], twist_ref[:, B:PAIR]
    for c in range(CH):
        rows, lanes = slice(B * c, B * c + B), slice(B * c, B * c + B)
        re, im = back[rows, 0:B], back[rows, B:PAIR]
        for at, part in ((0, re * cos + im * sin), (B, im * cos - re * sin)):
            high, low = split(part)
            tall[at : at + B, lanes] = high
            tall[PAIR + at : PAIR + at + B, lanes] = low
            tall[2 * PAIR + at : 2 * PAIR + at + B, lanes] = high
    return dot(out_of_ref[...], tall[...])


def filter_kernel(h_ref, into_ref, down_ref, twist_ref, o_ref, wide):
    parts = [split(h_ref[pl.ds(c, B, stride=CH), :]) for c in range(CH)]
    high = jnp.concatenate([p[0] for p in parts], axis=1)
    low = jnp.concatenate([p[1] for p in parts], axis=1)
    first = dot(into_ref[...], jnp.concatenate((high, high), axis=0)) + dot(into_ref[:, 0:B], low)
    spectrum(first, (down_ref, twist_ref), wide, o_ref)


WIDE = pltpu.VMEM((CH * B, 3 * PAIR), BF16)
TALL = pltpu.VMEM((3 * PAIR, CH * B), BF16)
BACK = pltpu.VMEM((CH * B, PAIR), F32)


def call(kernel, out_shape, name, flops, scratch_shapes=(), smem=0, inputs=0):
    vmem = pl.BlockSpec(memory_space=pltpu.VMEM)
    return pl.pallas_call(
        kernel,
        in_specs=[pl.BlockSpec(memory_space=pltpu.SMEM)] * smem + [vmem] * inputs,
        out_specs=jax.tree.map(lambda _: vmem, out_shape),
        out_shape=out_shape,
        scratch_shapes=scratch_shapes,
        compiler_params=pltpu.CompilerParams(vmem_limit_bytes=16 << 20),
        cost_estimate=pl.CostEstimate(flops=flops, transcendentals=0, bytes_accessed=2**21),
        name=name,
    )


SPECTRA = jax.ShapeDtypeStruct((CH * B, PAIR), F32)


def filter_spectra(h, into, down, twist):
    return call(filter_kernel, SPECTRA, "filter_spectra", 10**10, [WIDE], inputs=4)(
        h, into, down, twist
    )


def long_kernel(
    w_ref, kv_ref, h_ref, into_ref, down_ref, up_ref, out_of_ref, twist_ref, y_ref, z_ref, *scratch
):
    kvf, yf, wide, tall, back = scratch
    kvf[...] = kv_ref[...].astype(F32)
    row, lane = iota2((B, B), 0), iota2((B, B), 1)
    mine = CH * lax.axis_index("seq")

    def short(stream, c):
        x = kvf[pl.ds(CH * stream + c, B, stride=2 * CH), :]
        before = jnp.where(row == 0, 0.0, pltpu.roll(x, 1, 0))
        out = w_ref[stream + 1, 0, mine + c] * x
        for lag in (1, 2):
            moved = pltpu.roll(jnp.where(lane < B - lag, x, before), lag, 1)
            out = out + w_ref[stream + 1, lag, mine + c] * moved
        return out

    gated = [(short(0, c) * short(1, c)).astype(BF16) for c in range(CH)]
    gated = jnp.concatenate(gated, axis=1)
    first = dot(into_ref[...], jnp.concatenate((gated, gated), axis=0))
    spectrum(first, (down_ref, twist_ref), wide, z_ref)
    for c in range(CH):
        rows = slice(B * c, B * c + B)
        re, im = z_ref[rows, 0:B], z_ref[rows, B:PAIR]
        hre, him = h_ref[rows, 0:B], h_ref[rows, B:PAIR]
        stage(wide, rows, re * hre - im * him, re * him + im * hre)
    y = sequence(wide, back, tall, up_ref, out_of_ref, twist_ref)
    for c in range(CH):
        yf[pl.ds(c, B, stride=CH), :] = y[:, B * c : B * c + B]
    y_ref[...] = yf[...].astype(BF16)


def long_conv(w, kv, spectra, constants):
    into, down, up, out_of, twist = constants
    out_shape = [jax.ShapeDtypeStruct((CH * B, B), BF16), SPECTRA]
    scratch = [pltpu.VMEM((8 * B, B), F32), pltpu.VMEM((CH * B, B), F32), WIDE, TALL, BACK]
    return call(long_kernel, out_shape, "long_conv", 10**10, scratch, smem=1, inputs=7)(
        w, kv, spectra, into, down, up, out_of, twist
    )


def grad_kernel(
    back_ref, q_ref, z_ref, into_ref, down_ref, up_ref, out_of_ref, twist_ref, o_ref, f_ref, *scratch
):
    backf, yf, wide, tall, back = scratch
    backf[...] = back_ref[...].astype(F32)
    dy = [backf[pl.ds(CH + c, B, stride=2 * CH), :].astype(BF16) for c in range(CH)]
    dy = jnp.concatenate(dy, axis=1)
    first = dot(into_ref[...], jnp.concatenate((dy, dy), axis=0))
    spectrum(first, (down_ref, twist_ref), wide, back)
    for c in range(CH):
        rows = slice(B * c, B * c + B)
        re, im = back[rows, 0:B], back[rows, B:PAIR]
        zre, zim = z_ref[rows, 0:B], z_ref[rows, B:PAIR]
        stage(wide, rows, re * zre + im * zim, im * zre - re * zim)
    grad = sequence(wide, back, tall, up_ref, out_of_ref, twist_ref)
    for c in range(CH):
        f_ref[pl.ds(c, B, stride=CH), :] = grad[:, B * c : B * c + B]
    for c in range(CH):
        yf[pl.ds(c, B, stride=CH), :] = backf[pl.ds(c, B, stride=2 * CH), :]
    for g in range(CH):
        part = slice(B * g, B * g + B)
        o_ref[:, part] = (yf[part, :] * q_ref[part, :]).T.astype(BF16)


def grad_conv(back, q_conv_t, spectra, constants):
    into, down, up, out_of, twist = constants
    out_shape = [
        jax.ShapeDtypeStruct((B, CH * B), BF16),
        jax.ShapeDtypeStruct((CH * B, B), F32),
    ]
    scratch = [pltpu.VMEM((8 * B, B), F32), pltpu.VMEM((CH * B, B), F32), WIDE, TALL, BACK]
    return call(grad_kernel, out_shape, "grad_conv", 3 * 10**9, scratch, inputs=8)(
        back, q_conv_t, spectra, into, down, up, out_of, twist
    )


def query_kernel(w_ref, q_ref, tail_ref, o_ref, qf):
    tokens = q_ref.shape[0]
    qf[0:TAIL, :] = tail_ref[...].astype(F32)
    qf[TAIL : TAIL + tokens, :] = q_ref[...].astype(F32)
    out = w_ref[0, 0:1, :] * qf[TAIL : TAIL + tokens, :]
    for lag in (1, 2):
        out = out + w_ref[0, lag : lag + 1, :] * qf[TAIL - lag : TAIL - lag + tokens, :]
    for g in range(CH):
        part = slice(B * g, B * g + B)
        o_ref[part, :] = out[:, part].T


def query_conv(w, q, tail):
    tokens, width = q.shape
    out_shape = jax.ShapeDtypeStruct((width, tokens), F32)
    scratch = [pltpu.VMEM((TAIL + tokens, width), F32)]
    return call(query_kernel, out_shape, "query_conv", 10**10, scratch, inputs=3)(w, q, tail)


def homes(z):
    side = 1 - 2 * lax.rem(z, 2)
    moved = (0, 1, -1, -2, 2, 3, -3, -4)
    return [lax.rem(z + steps * side + 16, 8) for steps in moved]


def products(w_ref, sources, refs):
    blocks = []
    for ref in refs:
        blocks += [ref[at : at + B, :] for at in range(0, ref.shape[0], B)]
    total = None
    for source, block in zip(sources, blocks, strict=True):
        width = block.shape[1]
        start = pl.multiple_of(source * width, B)
        part = lax.dot_general(w_ref[:, pl.ds(start, width)], block, NT, preferred_element_type=F32)
        total = part if total is None else total + part
    return total


def early_kernel(w_ref, a_ref, b_ref, c_ref, d_ref, o_ref):
    o_ref[...] = products(w_ref, homes(lax.axis_index("chan"))[:6], (a_ref, b_ref, c_ref, d_ref))


def project_early(weight, *blocks):
    out_shape = jax.ShapeDtypeStruct((CH * B, B), F32)
    return call(early_kernel, out_shape, "project_early", 10**9, inputs=5)(weight, *blocks)


def project_kernel(w_ref, p_ref, e_ref, q_ref, y_ref, o_ref, df, yf, of):
    late = products(w_ref, homes(lax.axis_index("chan"))[6:], (e_ref,))
    df[...] = (p_ref[...] + late) * q_ref[...]
    yf[...] = y_ref[...].astype(F32)
    for c in range(CH):
        of[pl.ds(c, B, stride=2 * CH), :] = yf[pl.ds(c, B, stride=CH), :]
        of[pl.ds(CH + c, B, stride=2 * CH), :] = df[pl.ds(c, B, stride=CH), :]
    o_ref[...] = of[...].astype(BF16)


def project(weight, partial, last, q_conv_t, y):
    out_shape = jax.ShapeDtypeStruct((8 * B, B), BF16)
    scratch = [pltpu.VMEM((rows * B, B), F32) for rows in (CH, CH, 2 * CH)]
    return call(project_kernel, out_shape, "project", 10**9, scratch, inputs=5)(
        weight, partial, last, q_conv_t, y
    )


def exchange(value, axis):
    return lax.all_to_all(value, axis, split_axis=0, concat_axis=0, tiled=True)


INNER = [(i, i ^ 1) for i in range(8)]
OUTER = [(i, (i + 1 if i % 2 else i - 1) % 8) for i in range(8)]
SECOND = [(i, (i + 2 if i % 2 else i - 2) % 8) for i in range(8)]


def on_device(q_in, k_in, v_in, short_filters, long_filter, out_weight, out_grad):
    tokens, width = q_in.shape
    seq = lax.axis_size("seq")
    tie = lax.optimization_barrier

    r1 = lax.ppermute(out_grad, "chan", INNER)
    kv, tail = spread(k_in, v_in, q_in)
    before = lax.ppermute(tail, "seq", [(i, i + 1) for i in range(seq - 1)])
    kv, r1 = tie((kv, r1))
    pair = jnp.concatenate((out_grad, r1), axis=0)
    r2 = lax.ppermute(pair, "chan", OUTER)
    r3 = lax.ppermute(pair, "chan", SECOND)
    kv = exchange(kv.reshape(seq, 2 * CH, tokens), "seq")
    r2, r3, long_filter = tie((r2, r3, long_filter))
    r4 = lax.ppermute(r3, "chan", OUTER)

    constants = [jnp.asarray(table) for table in tables()]
    into, down, _, _, twist = constants
    h = long_filter.reshape(CH, B, B).transpose(1, 0, 2).reshape(CH * B, B)
    h_spectra = filter_spectra(h, into, down, twist)
    kv = kv.reshape(2 * CH * seq, tokens)
    y, z_spectra = long_conv(short_filters, kv, h_spectra, constants)
    q_conv_t = query_conv(short_filters, q_in, before)
    partial = project_early(out_weight, out_grad, r1, r2, tie((r3, y))[0])
    both = project(out_weight, partial, r4, q_conv_t, y)
    back = exchange(both.reshape(seq, 2 * CH, tokens), "seq").reshape(2 * CH * seq, tokens)
    operator_out, filter_grad = grad_conv(back, q_conv_t, z_spectra, constants)
    filter_grad = filter_grad.reshape(B, CH, B).transpose(1, 0, 2)
    return operator_out, filter_grad.reshape(1, CH, B * B)


def solution(mesh):
    in_specs = (
        P("seq", "chan"),
        P("seq", "chan"),
        P("seq", "chan"),
        P(None, None, "chan"),
        P("chan", "seq", None),
        P("chan", None),
        P("seq", "chan"),
    )
    out_specs = (P("seq", "chan"), P("chan", "seq", None))
    return jax.shard_map(
        on_device, mesh=mesh, in_specs=in_specs, out_specs=out_specs, check_vma=False
    )
```

```python
import jax
import jax.numpy as jnp
from jax import lax
from jax.experimental import pallas as pl
from jax.experimental.pallas import tpu as pltpu
import ml_dtypes
import numpy as np
from jax.sharding import PartitionSpec as P

F32 = jnp.float32
BF16 = jnp.bfloat16
B = 128
PAIR = 2 * B
CH = 4
TAIL = 16
NT = (((1,), (1,)), ((), ()))


def iota2(shape, dim):
    return lax.broadcasted_iota(jnp.int32, shape, dim)


def spread_kernel(k_ref, v_ref, q_ref, o_ref, tail_ref):
    tail_ref[...] = q_ref[...]
    row, col = iota2((PAIR, PAIR), 0), iota2((PAIR, PAIR), 1)
    source = (row // CH) % 2 * B + row // (2 * CH) * CH + row % CH
    pick = (col == source).astype(BF16)
    for g in range(4):
        lanes = slice(B * g, B * g + B)
        both = jnp.concatenate((k_ref[:, lanes], v_ref[:, lanes]), axis=1)
        rows = lax.dot_general(pick, both, NT, preferred_element_type=F32)
        o_ref[PAIR * g : PAIR * g + PAIR, :] = rows.astype(BF16)


def spread(k, v, q):
    tokens, width = k.shape
    whole = lambda *shape: pl.BlockSpec(shape, lambda i: (0, 0))
    return pl.pallas_call(
        spread_kernel,
        grid=(1,),
        in_specs=[
            whole(tokens, width),
            whole(tokens, width),
            pl.BlockSpec((TAIL, width), lambda i: (tokens // TAIL - 1, 0)),
        ],
        out_specs=[whole(2 * width, tokens), whole(TAIL, width)],
        out_shape=[
            jax.ShapeDtypeStruct((2 * width, tokens), BF16),
            jax.ShapeDtypeStruct((TAIL, width), BF16),
        ],
        cost_estimate=pl.CostEstimate(flops=10**9, transcendentals=0, bytes_accessed=2**20),
        name="spread",
    )(k, v, q)


def tables():
    def halves(x):
        high = x.astype(np.float32).astype(ml_dtypes.bfloat16)
        return high, (x - high.astype(np.float64)).astype(np.float32).astype(ml_dtypes.bfloat16)

    n = np.arange(B, dtype=np.float64)
    coarse = 2 * np.pi * (n[:, None] + 0.25) * n[None, :] / B
    turn = 2 * np.pi * (n[:, None] + 0.25) * n[None, :] / (B * B)
    fine = 2 * np.pi * (n[:, None] * n[None, :] % B) / B
    first = np.concatenate((np.cos(coarse), -np.sin(coarse)), 0)
    high, low = halves(first)
    into = np.concatenate((high, low), 1)
    high, low = halves(first.T / (B * B))
    out_of = np.concatenate((high, high, low), 1)
    cos, sin = np.cos(fine), np.sin(fine)
    high, low = halves(np.block([[cos, -sin], [sin, cos]]))
    down = np.concatenate((high, high, low), 0)
    high, low = halves(np.block([[cos, sin], [-sin, cos]]))
    up = np.concatenate((high, high, low), 0)
    twist = np.concatenate((np.cos(turn), -np.sin(turn)), 1).astype(np.float32)
    return into, down, up, out_of, twist


def split(x):
    high = x.astype(BF16)
    return high, (x - high.astype(F32)).astype(BF16)


def dot(x, y):
    return jnp.dot(x, y, preferred_element_type=F32)


def spectrum(first, into_refs, wide, spec_ref):
    down_ref, twist_ref = into_refs
    cos, sin = twist_ref[:, 0:B], twist_ref[:, B:PAIR]
    for c in range(CH):
        lanes, rows = slice(B * c, B * c + B), slice(B * c, B * c + B)
        re, im = first[0:B, lanes], first[B:PAIR, lanes]
        stage(wide, rows, re * cos - im * sin, re * sin + im * cos)
    spec_ref[...] = dot(wide[...], down_ref[...])


def stage(wide, rows, re, im):
    for at, part in ((0, re), (B, im)):
        high, low = split(part)
        wide[rows, at : at + B] = high
        wide[rows, PAIR + at : PAIR + at + B] = low
        wide[rows, 2 * PAIR + at : 2 * PAIR + at + B] = high


def sequence(wide, back, tall, up_ref, out_of_ref, twist_ref):
    back[...] = dot(wide[...], up_ref[...])
    cos, sin = twist_ref[:, 0:B], twist_ref[:, B:PAIR]
    for c in range(CH):
        rows, lanes = slice(B * c, B * c + B), slice(B * c, B * c + B)
        re, im = back[rows, 0:B], back[rows, B:PAIR]
        for at, part in ((0, re * cos + im * sin), (B, im * cos - re * sin)):
            high, low = split(part)
            tall[at : at + B, lanes] = high
            tall[PAIR + at : PAIR + at + B, lanes] = low
            tall[2 * PAIR + at : 2 * PAIR + at + B, lanes] = high
    return dot(out_of_ref[...], tall[...])


def filter_kernel(h_ref, into_ref, down_ref, twist_ref, o_ref, wide):
    parts = [split(h_ref[pl.ds(c, B, stride=CH), :]) for c in range(CH)]
    high = jnp.concatenate([p[0] for p in parts], axis=1)
    low = jnp.concatenate([p[1] for p in parts], axis=1)
    first = dot(into_ref[...], jnp.concatenate((high, high), axis=0)) + dot(into_ref[:, 0:B], low)
    spectrum(first, (down_ref, twist_ref), wide, o_ref)


WIDE = pltpu.VMEM((CH * B, 3 * PAIR), BF16)
TALL = pltpu.VMEM((3 * PAIR, CH * B), BF16)
BACK = pltpu.VMEM((CH * B, PAIR), F32)


def call(kernel, out_shape, name, flops, scratch_shapes=(), smem=0, inputs=0):
    vmem = pl.BlockSpec(memory_space=pltpu.VMEM)
    return pl.pallas_call(
        kernel,
        in_specs=[pl.BlockSpec(memory_space=pltpu.SMEM)] * smem + [vmem] * inputs,
        out_specs=jax.tree.map(lambda _: vmem, out_shape),
        out_shape=out_shape,
        scratch_shapes=scratch_shapes,
        compiler_params=pltpu.CompilerParams(vmem_limit_bytes=16 << 20),
        cost_estimate=pl.CostEstimate(flops=flops, transcendentals=0, bytes_accessed=2**21),
        name=name,
    )


SPECTRA = jax.ShapeDtypeStruct((CH * B, PAIR), F32)


def filter_spectra(h, into, down, twist):
    return call(filter_kernel, SPECTRA, "filter_spectra", 100000000, [WIDE], inputs=4)(
        h, into, down, twist
    )


def long_kernel(
    w_ref, kv_ref, h_ref, into_ref, down_ref, up_ref, out_of_ref, twist_ref, y_ref, z_ref, *scratch
):
    kvf, yf, wide, tall, back = scratch
    kvf[...] = kv_ref[...].astype(F32)
    row, lane = iota2((B, B), 0), iota2((B, B), 1)
    mine = CH * lax.axis_index("seq")

    def short(stream, c):
        x = kvf[pl.ds(CH * stream + c, B, stride=2 * CH), :]
        before = jnp.where(row == 0, 0.0, pltpu.roll(x, 1, 0))
        out = w_ref[stream + 1, 0, mine + c] * x
        for lag in (1, 2):
            moved = pltpu.roll(jnp.where(lane < B - lag, x, before), lag, 1)
            out = out + w_ref[stream + 1, lag, mine + c] * moved
        return out

    gated = [(short(0, c) * short(1, c)).astype(BF16) for c in range(CH)]
    gated = jnp.concatenate(gated, axis=1)
    first = dot(into_ref[...], jnp.concatenate((gated, gated), axis=0))
    spectrum(first, (down_ref, twist_ref), wide, z_ref)
    for c in range(CH):
        rows = slice(B * c, B * c + B)
        re, im = z_ref[rows, 0:B], z_ref[rows, B:PAIR]
        hre, him = h_ref[rows, 0:B], h_ref[rows, B:PAIR]
        stage(wide, rows, re * hre - im * him, re * him + im * hre)
    y = sequence(wide, back, tall, up_ref, out_of_ref, twist_ref)
    for c in range(CH):
        yf[pl.ds(c, B, stride=CH), :] = y[:, B * c : B * c + B]
    y_ref[...] = yf[...].astype(BF16)


def long_conv(w, kv, spectra, constants):
    into, down, up, out_of, twist = constants
    out_shape = [jax.ShapeDtypeStruct((CH * B, B), BF16), SPECTRA]
    scratch = [pltpu.VMEM((8 * B, B), F32), pltpu.VMEM((CH * B, B), F32), WIDE, TALL, BACK]
    return call(long_kernel, out_shape, "long_conv", 100000000, scratch, smem=1, inputs=7)(
        w, kv, spectra, into, down, up, out_of, twist
    )


def grad_kernel(
    back_ref, q_ref, z_ref, into_ref, down_ref, up_ref, out_of_ref, twist_ref, o_ref, f_ref, *scratch
):
    backf, yf, wide, tall, back = scratch
    backf[...] = back_ref[...].astype(F32)
    dy = [backf[pl.ds(CH + c, B, stride=2 * CH), :].astype(BF16) for c in range(CH)]
    dy = jnp.concatenate(dy, axis=1)
    first = dot(into_ref[...], jnp.concatenate((dy, dy), axis=0))
    spectrum(first, (down_ref, twist_ref), wide, back)
    for c in range(CH):
        rows = slice(B * c, B * c + B)
        re, im = back[rows, 0:B], back[rows, B:PAIR]
        zre, zim = z_ref[rows, 0:B], z_ref[rows, B:PAIR]
        stage(wide, rows, re * zre + im * zim, im * zre - re * zim)
    grad = sequence(wide, back, tall, up_ref, out_of_ref, twist_ref)
    for c in range(CH):
        f_ref[pl.ds(c, B, stride=CH), :] = grad[:, B * c : B * c + B]
    for c in range(CH):
        yf[pl.ds(c, B, stride=CH), :] = backf[pl.ds(c, B, stride=2 * CH), :]
    for g in range(CH):
        part = slice(B * g, B * g + B)
        o_ref[:, part] = (yf[part, :] * q_ref[part, :]).T.astype(BF16)


def grad_conv(back, q_conv_t, spectra, constants):
    into, down, up, out_of, twist = constants
    out_shape = [
        jax.ShapeDtypeStruct((B, CH * B), BF16),
        jax.ShapeDtypeStruct((CH * B, B), F32),
    ]
    scratch = [pltpu.VMEM((8 * B, B), F32), pltpu.VMEM((CH * B, B), F32), WIDE, TALL, BACK]
    return call(grad_kernel, out_shape, "grad_conv", 3 * 10**9, scratch, inputs=8)(
        back, q_conv_t, spectra, into, down, up, out_of, twist
    )


def query_kernel(w_ref, q_ref, tail_ref, o_ref, qf):
    tokens = q_ref.shape[0]
    qf[0:TAIL, :] = tail_ref[...].astype(F32)
    qf[TAIL : TAIL + tokens, :] = q_ref[...].astype(F32)
    out = w_ref[0, 0:1, :] * qf[TAIL : TAIL + tokens, :]
    for lag in (1, 2):
        out = out + w_ref[0, lag : lag + 1, :] * qf[TAIL - lag : TAIL - lag + tokens, :]
    for g in range(CH):
        part = slice(B * g, B * g + B)
        o_ref[part, :] = out[:, part].T


def query_conv(w, q, tail):
    tokens, width = q.shape
    out_shape = jax.ShapeDtypeStruct((width, tokens), F32)
    scratch = [pltpu.VMEM((TAIL + tokens, width), F32)]
    return call(query_kernel, out_shape, "query_conv", 100000000, scratch, inputs=3)(w, q, tail)


def products(w_ref, steps, blocks):
    z = lax.axis_index("chan")
    total = None
    for step, block in zip(steps, blocks, strict=True):
        width = block.shape[1]
        start = pl.multiple_of(lax.rem(z + step + 8, 8) * width, B)
        part = lax.dot_general(w_ref[:, pl.ds(start, width)], block, NT, preferred_element_type=F32)
        total = part if total is None else total + part
    return total


def early_kernel(w_ref, own_ref, up1_ref, down1_ref, up2_ref, down2_ref, o_ref):
    refs = (own_ref, up1_ref, down1_ref, up2_ref, down2_ref)
    o_ref[...] = products(w_ref, (0, 1, -1, 2, -2), [ref[...] for ref in refs])


def project_early(weight, *blocks):
    out_shape = jax.ShapeDtypeStruct((CH * B, B), F32)
    return call(early_kernel, out_shape, "project_early", 10**9, inputs=6)(weight, *blocks)


def project_kernel(w_ref, p_ref, up_ref, down_ref, q_ref, y_ref, o_ref, df, yf, of):
    far = jnp.concatenate((up_ref[B:, :], down_ref[B:, :]), axis=0)
    late = products(w_ref, (3, -3, 4), [up_ref[0:B, :], down_ref[0:B, :], far])
    df[...] = (p_ref[...] + late) * q_ref[...]
    yf[...] = y_ref[...].astype(F32)
    for c in range(CH):
        of[pl.ds(c, B, stride=2 * CH), :] = yf[pl.ds(c, B, stride=CH), :]
        of[pl.ds(CH + c, B, stride=2 * CH), :] = df[pl.ds(c, B, stride=CH), :]
    o_ref[...] = of[...].astype(BF16)


def project(weight, partial, up, down, q_conv_t, y):
    out_shape = jax.ShapeDtypeStruct((8 * B, B), BF16)
    scratch = [pltpu.VMEM((rows * B, B), F32) for rows in (CH, CH, 2 * CH)]
    return call(project_kernel, out_shape, "project", 10**9, scratch, inputs=6)(
        weight, partial, up, down, q_conv_t, y
    )


def exchange(value, axis):
    return lax.all_to_all(value, axis, split_axis=0, concat_axis=0, tiled=True)


def bring(value, steps):
    return lax.ppermute(value, "chan", [(i, (i - steps) % 8) for i in range(8)])


def on_device(q_in, k_in, v_in, short_filters, long_filter, out_weight, out_grad):
    tokens, width = q_in.shape
    seq = lax.axis_size("seq")
    tie = lax.optimization_barrier

    kv, tail = spread(k_in, v_in, q_in)
    kv, out_grad = tie((kv, out_grad))
    kv = exchange(kv.reshape(seq, 2 * CH, tokens), "seq")

    up2, down2, up1, down1 = (bring(out_grad, steps) for steps in (2, -2, 1, -1))
    half = tokens // 2
    up1, down1, up2, down2, tail, long_filter = tie((up1, down1, up2, down2, tail, long_filter))
    above = bring(jnp.concatenate((up1, up2[:half]), axis=0), 2)
    below = bring(jnp.concatenate((down1, down2[half:]), axis=0), -2)
    before = lax.ppermute(tail, "seq", [(i, i + 1) for i in range(seq - 1)])

    constants = [jnp.asarray(table) for table in tables()]
    into, down, _, _, twist = constants
    h = long_filter.reshape(CH, B, B).transpose(1, 0, 2).reshape(CH * B, B)
    h_spectra = filter_spectra(h, into, down, twist)
    kv = kv.reshape(2 * CH * seq, tokens)
    y, z_spectra = long_conv(short_filters, kv, h_spectra, constants)
    q_conv_t = query_conv(short_filters, q_in, before)
    partial = project_early(out_weight, out_grad, up1, down1, up2, tie((down2, y))[0])
    both = project(out_weight, partial, above, below, q_conv_t, y)
    back = exchange(both.reshape(seq, 2 * CH, tokens), "seq").reshape(2 * CH * seq, tokens)
    operator_out, filter_grad = grad_conv(back, q_conv_t, z_spectra, constants)
    filter_grad = filter_grad.reshape(B, CH, B).transpose(1, 0, 2)
    return operator_out, filter_grad.reshape(1, CH, B * B)


def solution(mesh):
    in_specs = (
        P("seq", "chan"),
        P("seq", "chan"),
        P("seq", "chan"),
        P(None, None, "chan"),
        P("chan", "seq", None),
        P("chan", None),
        P("seq", "chan"),
    )
    out_specs = (P("seq", "chan"), P("chan", "seq", None))
    return jax.shard_map(
        on_device, mesh=mesh, in_specs=in_specs, out_specs=out_specs, check_vma=False
    )
```

```python
import jax
import jax.numpy as jnp
from jax import lax
from jax.experimental import pallas as pl
from jax.experimental.pallas import tpu as pltpu
import ml_dtypes
import numpy as np
from jax.sharding import PartitionSpec as P

F32 = jnp.float32
BF16 = jnp.bfloat16
B = 128
PAIR = 2 * B
CH = 4
TAIL = 16
NT = (((1,), (1,)), ((), ()))


def iota2(shape, dim):
    return lax.broadcasted_iota(jnp.int32, shape, dim)


def spread_kernel(k_ref, v_ref, q_ref, o_ref, tail_ref):
    tail_ref[...] = q_ref[...]
    row, col = iota2((PAIR, PAIR), 0), iota2((PAIR, PAIR), 1)
    source = (row // CH) % 2 * B + row // (2 * CH) * CH + row % CH
    pick = (col == source).astype(BF16)
    for g in range(4):
        lanes = slice(B * g, B * g + B)
        both = jnp.concatenate((k_ref[:, lanes], v_ref[:, lanes]), axis=1)
        rows = lax.dot_general(pick, both, NT, preferred_element_type=F32)
        o_ref[PAIR * g : PAIR * g + PAIR, :] = rows.astype(BF16)


def spread(k, v, q):
    tokens, width = k.shape
    whole = lambda *shape: pl.BlockSpec(shape, lambda i: (0, 0))
    return pl.pallas_call(
        spread_kernel,
        grid=(1,),
        in_specs=[
            whole(tokens, width),
            whole(tokens, width),
            pl.BlockSpec((TAIL, width), lambda i: (tokens // TAIL - 1, 0)),
        ],
        out_specs=[whole(2 * width, tokens), whole(TAIL, width)],
        out_shape=[
            jax.ShapeDtypeStruct((2 * width, tokens), BF16),
            jax.ShapeDtypeStruct((TAIL, width), BF16),
        ],
        cost_estimate=pl.CostEstimate(flops=10**9, transcendentals=0, bytes_accessed=2**20),
        name="spread",
    )(k, v, q)


def tables():
    def halves(x):
        high = x.astype(np.float32).astype(ml_dtypes.bfloat16)
        return high, (x - high.astype(np.float64)).astype(np.float32).astype(ml_dtypes.bfloat16)

    n = np.arange(B, dtype=np.float64)
    coarse = 2 * np.pi * (n[:, None] + 0.25) * n[None, :] / B
    turn = 2 * np.pi * (n[:, None] + 0.25) * n[None, :] / (B * B)
    fine = 2 * np.pi * (n[:, None] * n[None, :] % B) / B
    first = np.concatenate((np.cos(coarse), -np.sin(coarse)), 0)
    high, low = halves(first)
    into = np.concatenate((high, low), 1)
    high, low = halves(first.T / (B * B))
    out_of = np.concatenate((high, high, low), 1)
    cos, sin = np.cos(fine), np.sin(fine)
    high, low = halves(np.block([[cos, -sin], [sin, cos]]))
    down = np.concatenate((high, high, low), 0)
    high, low = halves(np.block([[cos, sin], [-sin, cos]]))
    up = np.concatenate((high, high, low), 0)
    twist = np.concatenate((np.cos(turn), -np.sin(turn)), 1).astype(np.float32)
    return into, down, up, out_of, twist


def split(x):
    high = x.astype(BF16)
    return high, (x - high.astype(F32)).astype(BF16)


def dot(x, y):
    return jnp.dot(x, y, preferred_element_type=F32)


def spectrum(first, into_refs, wide, spec_ref):
    down_ref, twist_ref = into_refs
    cos, sin = twist_ref[:, 0:B], twist_ref[:, B:PAIR]
    for c in range(CH):
        lanes, rows = slice(B * c, B * c + B), slice(B * c, B * c + B)
        re, im = first[0:B, lanes], first[B:PAIR, lanes]
        stage(wide, rows, re * cos - im * sin, re * sin + im * cos)
    spec_ref[...] = dot(wide[...], down_ref[...])


def stage(wide, rows, re, im):
    for at, part in ((0, re), (B, im)):
        high, low = split(part)
        wide[rows, at : at + B] = high
        wide[rows, PAIR + at : PAIR + at + B] = low
        wide[rows, 2 * PAIR + at : 2 * PAIR + at + B] = high


def sequence(wide, back, tall, up_ref, out_of_ref, twist_ref):
    back[...] = dot(wide[...], up_ref[...])
    cos, sin = twist_ref[:, 0:B], twist_ref[:, B:PAIR]
    for c in range(CH):
        rows, lanes = slice(B * c, B * c + B), slice(B * c, B * c + B)
        re, im = back[rows, 0:B], back[rows, B:PAIR]
        for at, part in ((0, re * cos + im * sin), (B, im * cos - re * sin)):
            high, low = split(part)
            tall[at : at + B, lanes] = high
            tall[PAIR + at : PAIR + at + B, lanes] = low
            tall[2 * PAIR + at : 2 * PAIR + at + B, lanes] = high
    return dot(out_of_ref[...], tall[...])


def filter_kernel(h_ref, into_ref, down_ref, twist_ref, o_ref, wide):
    parts = [split(h_ref[pl.ds(c, B, stride=CH), :]) for c in range(CH)]
    high = jnp.concatenate([p[0] for p in parts], axis=1)
    low = jnp.concatenate([p[1] for p in parts], axis=1)
    first = dot(into_ref[...], jnp.concatenate((high, high), axis=0)) + dot(into_ref[:, 0:B], low)
    spectrum(first, (down_ref, twist_ref), wide, o_ref)


WIDE = pltpu.VMEM((CH * B, 3 * PAIR), BF16)
TALL = pltpu.VMEM((3 * PAIR, CH * B), BF16)
BACK = pltpu.VMEM((CH * B, PAIR), F32)


def call(kernel, out_shape, name, flops, scratch_shapes=(), smem=0, inputs=0):
    vmem = pl.BlockSpec(memory_space=pltpu.VMEM)
    return pl.pallas_call(
        kernel,
        in_specs=[pl.BlockSpec(memory_space=pltpu.SMEM)] * smem + [vmem] * inputs,
        out_specs=jax.tree.map(lambda _: vmem, out_shape),
        out_shape=out_shape,
        scratch_shapes=scratch_shapes,
        compiler_params=pltpu.CompilerParams(vmem_limit_bytes=16 << 20),
        cost_estimate=pl.CostEstimate(flops=flops, transcendentals=0, bytes_accessed=2**21),
        name=name,
    )


SPECTRA = jax.ShapeDtypeStruct((CH * B, PAIR), F32)


def filter_spectra(h, into, down, twist):
    return call(filter_kernel, SPECTRA, "filter_spectra", 10**10, [WIDE], inputs=4)(
        h, into, down, twist
    )


def long_kernel(
    w_ref, kv_ref, h_ref, into_ref, down_ref, up_ref, out_of_ref, twist_ref, y_ref, z_ref, *scratch
):
    kvf, yf, wide, tall, back = scratch
    kvf[...] = kv_ref[...].astype(F32)
    row, lane = iota2((B, B), 0), iota2((B, B), 1)
    mine = CH * lax.axis_index("seq")

    def short(stream, c):
        x = kvf[pl.ds(CH * stream + c, B, stride=2 * CH), :]
        before = jnp.where(row == 0, 0.0, pltpu.roll(x, 1, 0))
        out = w_ref[stream + 1, 0, mine + c] * x
        for lag in (1, 2):
            moved = pltpu.roll(jnp.where(lane < B - lag, x, before), lag, 1)
            out = out + w_ref[stream + 1, lag, mine + c] * moved
        return out

    gated = [(short(0, c) * short(1, c)).astype(BF16) for c in range(CH)]
    gated = jnp.concatenate(gated, axis=1)
    first = dot(into_ref[...], jnp.concatenate((gated, gated), axis=0))
    spectrum(first, (down_ref, twist_ref), wide, z_ref)
    for c in range(CH):
        rows = slice(B * c, B * c + B)
        re, im = z_ref[rows, 0:B], z_ref[rows, B:PAIR]
        hre, him = h_ref[rows, 0:B], h_ref[rows, B:PAIR]
        stage(wide, rows, re * hre - im * him, re * him + im * hre)
    y = sequence(wide, back, tall, up_ref, out_of_ref, twist_ref)
    for c in range(CH):
        yf[pl.ds(c, B, stride=CH), :] = y[:, B * c : B * c + B]
    y_ref[...] = yf[...].astype(BF16)


def long_conv(w, kv, spectra, constants):
    into, down, up, out_of, twist = constants
    out_shape = [jax.ShapeDtypeStruct((CH * B, B), BF16), SPECTRA]
    scratch = [pltpu.VMEM((8 * B, B), F32), pltpu.VMEM((CH * B, B), F32), WIDE, TALL, BACK]
    return call(long_kernel, out_shape, "long_conv", 10**10, scratch, smem=1, inputs=7)(
        w, kv, spectra, into, down, up, out_of, twist
    )


def grad_kernel(
    back_ref, q_ref, z_ref, into_ref, down_ref, up_ref, out_of_ref, twist_ref, o_ref, f_ref, *scratch
):
    backf, yf, wide, tall, back = scratch
    backf[...] = back_ref[...].astype(F32)
    for c in range(CH):
        yf[pl.ds(c, B, stride=CH), :] = backf[pl.ds(c, B, stride=2 * CH), :]
    for g in range(CH):
        part = slice(B * g, B * g + B)
        o_ref[:, part] = (yf[part, :] * q_ref[part, :]).T.astype(BF16)
    dy = [backf[pl.ds(CH + c, B, stride=2 * CH), :].astype(BF16) for c in range(CH)]
    dy = jnp.concatenate(dy, axis=1)
    first = dot(into_ref[...], jnp.concatenate((dy, dy), axis=0))
    spectrum(first, (down_ref, twist_ref), wide, back)
    for c in range(CH):
        rows = slice(B * c, B * c + B)
        re, im = back[rows, 0:B], back[rows, B:PAIR]
        zre, zim = z_ref[rows, 0:B], z_ref[rows, B:PAIR]
        stage(wide, rows, re * zre + im * zim, im * zre - re * zim)
    grad = sequence(wide, back, tall, up_ref, out_of_ref, twist_ref)
    for c in range(CH):
        f_ref[pl.ds(c, B, stride=CH), :] = grad[:, B * c : B * c + B]


def grad_conv(back, q_conv_t, spectra, constants):
    into, down, up, out_of, twist = constants
    out_shape = [
        jax.ShapeDtypeStruct((B, CH * B), BF16),
        jax.ShapeDtypeStruct((CH * B, B), F32),
    ]
    scratch = [pltpu.VMEM((8 * B, B), F32), pltpu.VMEM((CH * B, B), F32), WIDE, TALL, BACK]
    return call(grad_kernel, out_shape, "grad_conv", 3 * 10**9, scratch, inputs=8)(
        back, q_conv_t, spectra, into, down, up, out_of, twist
    )


def query_kernel(w_ref, q_ref, tail_ref, o_ref, qf):
    tokens = q_ref.shape[0]
    qf[0:TAIL, :] = tail_ref[...].astype(F32)
    qf[TAIL : TAIL + tokens, :] = q_ref[...].astype(F32)
    out = w_ref[0, 0:1, :] * qf[TAIL : TAIL + tokens, :]
    for lag in (1, 2):
        out = out + w_ref[0, lag : lag + 1, :] * qf[TAIL - lag : TAIL - lag + tokens, :]
    for g in range(CH):
        part = slice(B * g, B * g + B)
        o_ref[part, :] = out[:, part].T


def query_conv(w, q, tail):
    tokens, width = q.shape
    out_shape = jax.ShapeDtypeStruct((width, tokens), F32)
    scratch = [pltpu.VMEM((TAIL + tokens, width), F32)]
    return call(query_kernel, out_shape, "query_conv", 10**10, scratch, inputs=3)(w, q, tail)


def homes(z):
    side = 1 - 2 * lax.rem(z, 2)
    moved = (0, 1, -1, -2, 2, 3, -3, -4)
    return [lax.rem(z + steps * side + 16, 8) for steps in moved]


def products(w_ref, sources, refs):
    blocks = []
    for ref in refs:
        blocks += [ref[at : at + B, :] for at in range(0, ref.shape[0], B)]
    total = None
    for source, block in zip(sources, blocks, strict=True):
        width = block.shape[1]
        start = pl.multiple_of(source * width, B)
        part = lax.dot_general(w_ref[:, pl.ds(start, width)], block, NT, preferred_element_type=F32)
        total = part if total is None else total + part
    return total


def early_kernel(w_ref, a_ref, b_ref, c_ref, d_ref, o_ref):
    o_ref[...] = products(w_ref, homes(lax.axis_index("chan"))[:6], (a_ref, b_ref, c_ref, d_ref))


def project_early(weight, *blocks):
    out_shape = jax.ShapeDtypeStruct((CH * B, B), F32)
    return call(early_kernel, out_shape, "project_early", 10**9, inputs=5)(weight, *blocks)


def project_kernel(w_ref, p_ref, e_ref, q_ref, y_ref, o_ref, df, yf, of):
    late = products(w_ref, homes(lax.axis_index("chan"))[6:], (e_ref,))
    df[...] = (p_ref[...] + late) * q_ref[...]
    yf[...] = y_ref[...].astype(F32)
    for c in range(CH):
        of[pl.ds(c, B, stride=2 * CH), :] = yf[pl.ds(c, B, stride=CH), :]
        of[pl.ds(CH + c, B, stride=2 * CH), :] = df[pl.ds(c, B, stride=CH), :]
    o_ref[...] = of[...].astype(BF16)


def project(weight, partial, last, q_conv_t, y):
    out_shape = jax.ShapeDtypeStruct((8 * B, B), BF16)
    scratch = [pltpu.VMEM((rows * B, B), F32) for rows in (CH, CH, 2 * CH)]
    return call(project_kernel, out_shape, "project", 10**9, scratch, inputs=5)(
        weight, partial, last, q_conv_t, y
    )


def exchange(value, axis):
    return lax.all_to_all(value, axis, split_axis=0, concat_axis=0, tiled=True)


INNER = [(i, i ^ 1) for i in range(8)]
OUTER = [(i, (i + 1 if i % 2 else i - 1) % 8) for i in range(8)]
SECOND = [(i, (i + 2 if i % 2 else i - 2) % 8) for i in range(8)]


def on_device(q_in, k_in, v_in, short_filters, long_filter, out_weight, out_grad):
    tokens, width = q_in.shape
    seq = lax.axis_size("seq")
    tie = lax.optimization_barrier

    r1 = lax.ppermute(out_grad, "chan", INNER)
    kv, tail = spread(k_in, v_in, q_in)
    before = lax.ppermute(tail, "seq", [(i, i + 1) for i in range(seq - 1)])
    kv, r1 = tie((kv, r1))
    pair = jnp.concatenate((out_grad, r1), axis=0)
    r2 = lax.ppermute(pair, "chan", OUTER)
    r3 = lax.ppermute(pair, "chan", SECOND)
    kv = exchange(kv.reshape(seq, 2 * CH, tokens), "seq")
    r2, r3, long_filter = tie((r2, r3, long_filter))
    r4 = lax.ppermute(r3, "chan", OUTER)

    constants = [jnp.asarray(table) for table in tables()]
    into, down, _, _, twist = constants
    h = long_filter.reshape(CH, B, B).transpose(1, 0, 2).reshape(CH * B, B)
    h_spectra = filter_spectra(h, into, down, twist)
    kv = kv.reshape(2 * CH * seq, tokens)
    y, z_spectra = long_conv(short_filters, kv, h_spectra, constants)
    q_conv_t = query_conv(short_filters, q_in, before)
    partial = project_early(out_weight, out_grad, r1, r2, tie((r3, y))[0])
    both = project(out_weight, partial, r4, q_conv_t, y)
    back = exchange(both.reshape(seq, 2 * CH, tokens), "seq").reshape(2 * CH * seq, tokens)
    operator_out, filter_grad = grad_conv(back, q_conv_t, z_spectra, constants)
    filter_grad = filter_grad.reshape(B, CH, B).transpose(1, 0, 2)
    return operator_out, filter_grad.reshape(1, CH, B * B)


def solution(mesh):
    in_specs = (
        P("seq", "chan"),
        P("seq", "chan"),
        P("seq", "chan"),
        P(None, None, "chan"),
        P("chan", "seq", None),
        P("chan", None),
        P("seq", "chan"),
    )
    out_specs = (P("seq", "chan"), P("chan", "seq", None))
    return jax.shard_map(
        on_device, mesh=mesh, in_specs=in_specs, out_specs=out_specs, check_vma=False
    )
```
